32 devices in a mesh: aux: 8 (over z, x), pair: 4 (over y, core).
Axes of the slice: x: 2, y: 2, z: 4, core: 2. Of those that a mesh axis runs over, the one named last changes fastest.
Arguments:
- three_center: float32 [8192, 4, 384], P('aux', 'pair'), may hold values from -0.875 to 0.875
- occ_energy: float32 [4], P('pair'), may hold values from -1.5 to -0.3
- vir_energy: float32 [384], replicated, may hold values from 0.2 to 3
- pair_mask: int32 [4, 4], replicated, may hold values from 0 to 1, as said below
Outputs:
- gamma_aux: float32 [8192, 4, 384], P('aux', 'pair')
The draws below stay inside these ranges and needn't reach their ends.
Inputs may be any that keep to these rules, and one draw needn't show every extreme that they name: pair_mask is symmetric and holds 1 on its diagonal.
All inputs are finite; a program needn't handle non-finite values.
Results may differ from the reference program's by a relative error of at most 0.000071.
Values sent between devices are 32-bit elements; how exact they have to be, the bound alone decides.
No kernel may reach another device: no remote copies, remote signals or barrier semaphores. Data moves between devices by JAX's collectives and lax.ppermute only.
A program may use at most 64 MiB of HBM per device.

```python
import jax
import jax.numpy as jnp
from jax import lax

VIR = 384
OCC_DEV = 1
NAUX = 8192
NOCC = 4


def draw_pair_mask(key, part):
    first_key, second_key = jax.random.split(jax.random.fold_in(key, 17))
    panel_count = NOCC // OCC_DEV
    levels = jax.random.randint(first_key, (panel_count,), 0, 4)
    orbital_panel = jnp.arange(NOCC, dtype=jnp.int32) // OCC_DEV
    level_rows = levels[orbital_panel]
    cutoff = level_rows[:, None] + level_rows[None, :]
    uniform_ints = jax.random.randint(second_key, (NOCC, NOCC), 0, 7)
    upper_part = (uniform_ints < cutoff).astype(jnp.int32)
    orbital_index = jnp.arange(NOCC, dtype=jnp.int32)
    symmetric = jnp.where(orbital_index[:, None] <= orbital_index[None, :], upper_part, upper_part.T)
    return jnp.where(orbital_index[:, None] == orbital_index[None, :], 1, symmetric).astype(jnp.int32)


def with_spikes(values, key, source, target, parts, factor):
    owner, partner = [(jnp.arange(values.shape[position]) // (values.shape[position] // parts)).reshape([-1 if axis == position else 1 for axis in range(values.ndim)]) for position in (source, target)]
    chosen = jax.random.permutation(key, parts)[partner]
    strong = (owner == chosen) | (owner == (partner + parts // 2) % parts)
    return jnp.where(strong, factor * values, values)


def steps_of(key, shape, cuts, least, top_value):
    def one(position, parts):
        heights = jax.random.uniform(jax.random.fold_in(jax.random.fold_in(key, 6), position), (parts,), jnp.float32, least / len(cuts), top_value / len(cuts))
        return jnp.repeat(jnp.exp(heights), shape[position] // parts).reshape((-1,) + (1,) * (len(shape) - position - 1))

    loudness = one(*cuts[0])
    for cut in cuts[1:]:
        loudness = loudness * one(*cut)
    return loudness


def bell_draw_with(own_key, shape, width, bound, cuts, heavy, kind=jnp.bfloat16):
    result = width * jax.random.normal(own_key, shape, jnp.float32)
    if cuts:
        result = result * steps_of(own_key, shape, cuts, -0.22, 0.18)
    return jnp.clip(with_spikes(result, jax.random.fold_in(own_key, 3), *heavy), -bound, bound).astype(kind)


def setup_inputs(seed: int = 0) -> dict:
    seeds = jax.random.split(jax.random.key(seed), 5)
    three_center = bell_draw_with(seeds[0], (NAUX, NOCC, VIR), (NAUX ** -0.25), 0.875, ((0, 8), (1, 4)), (0, 2, 8, 2.0), jnp.float32)
    occ_energy = jnp.clip(-1.5 + 1.2 * jax.random.uniform(seeds[1], (NOCC,), jnp.float32) ** steps_of(seeds[1], (NOCC,), ((0, 4),), -0.2, 0.2), -1.5, -0.3)
    vir_energy = jnp.clip(jax.random.uniform(seeds[2], (VIR,), jnp.float32, 0.2, 3.0), 0.2, 3.0)
    pair_mask = draw_pair_mask(jax.random.fold_in(seeds[4], 71), 0)
    return {"three_center": three_center, "occ_energy": occ_energy, "vir_energy": vir_energy, "pair_mask": pair_mask}


def reference(three_center, occ_energy, vir_energy, pair_mask):
    aux_total, occ_total, vir_total = three_center.shape
    flat_cols = occ_total * vir_total
    flattened = three_center.reshape(aux_total, flat_cols)
    pair_ints = jnp.dot(flattened.T, flattened, precision=lax.Precision.HIGHEST, preferred_element_type=jnp.float32)
    pair_ints = pair_ints.reshape(occ_total, vir_total, occ_total, vir_total)
    denominator = (vir_energy[None, :, None, None] + vir_energy[None, None, None, :]
                   - occ_energy[:, None, None, None] - occ_energy[None, None, :, None])
    weights = pair_mask.astype(jnp.float32)[:, None, :, None]
    amplitudes = (weights * pair_ints) / denominator
    amplitudes = amplitudes.reshape(flat_cols, flat_cols)
    gamma_aux = jnp.dot(flattened, amplitudes.T, precision=lax.Precision.HIGHEST, preferred_element_type=jnp.float32)
    return gamma_aux.reshape(aux_total, occ_total, vir_total)
```

```python
import jax
import jax.numpy as jnp
from jax import lax
from jax.sharding import PartitionSpec as P

AXES = ("aux", "pair")
precision = lax.Precision.HIGH


def across(value, aux_flip, pair_flip):
    aux_count, pair_count = lax.axis_size("aux"), lax.axis_size("pair")
    moves = [
        (a * pair_count + p, (a ^ aux_flip) * pair_count + (p ^ pair_flip))
        for a in range(aux_count)
        for p in range(pair_count)
    ]
    return lax.ppermute(value, AXES, moves)


def pick(pieces, index):
    return lax.dynamic_index_in_dim(pieces, index, 0, keepdims=False)


def tn(left, right):
    return lax.dot_general(
        left, right, (((0,), (0,)), ((), ())), precision=precision,
        preferred_element_type=jnp.float32)


def nt(left, right):
    return lax.dot_general(
        left, right, (((1,), (1,)), ((), ())), precision=precision,
        preferred_element_type=jnp.float32)


def nn(left, right):
    return jnp.dot(left, right, precision=precision, preferred_element_type=jnp.float32)


def scatter_sum(value, flips, index):
    members = len(flips)
    pieces = value.reshape((members, value.shape[0] // members) + value.shape[1:])
    total = pick(pieces, index)
    for step in range(1, members):
        total = total + across(pick(pieces, index ^ step), *flips[step])
    return total


def gather(piece, flips, index):
    members = len(flips)
    whole = jnp.zeros((members,) + piece.shape, piece.dtype)
    whole = lax.dynamic_update_index_in_dim(whole, piece, index, 0)
    for step in range(1, members):
        whole = lax.dynamic_update_index_in_dim(
            whole, across(piece, *flips[step]), index ^ step, 0)
    return whole.reshape((members * piece.shape[0],) + piece.shape[1:])


def aux_groups(aux_count):
    bits = aux_count.bit_length() - 1
    low, groups = 1, []
    while low < bits:
        width = min(2, bits - low)
        groups.append((low, width))
        low += width
    return groups


def on_device(three_center, occ_energy, vir_energy, pair_mask):
    rows, occ_count, virt = three_center.shape
    aux_count = lax.axis_size("aux")
    aux, pair = lax.axis_index("aux"), lax.axis_index("pair")
    side, lane = pair // 2, pair % 2
    half = rows // 2
    own = three_center.reshape(rows, virt)
    pieces = own.reshape(2, half, virt)
    occ_side = jnp.stack([occ_energy[0], across(occ_energy, 0, 1)[0]])
    occ_side = jnp.where(lane == 0, occ_side, occ_side[::-1])
    occ_other = across(occ_side, 0, 2)
    occ_low = jnp.where(side == 0, occ_side, occ_other)
    occ_high = jnp.where(side == 0, occ_other, occ_side)
    mask = pair_mask.astype(jnp.float32)

    facing_near = across(pick(pieces, side ^ 1), 0, 2)
    twin = across(own, 0, 1)
    facing_far = across(pick(pieces, side), 0, 2)

    z_groups = aux_groups(aux_count)

    def z_scatter(value):
        start = jnp.int32(0)
        for low, width in z_groups:
            members = 1 << width
            index = (aux >> low) & (members - 1)
            value = scatter_sum(value, [(s << low, 0) for s in range(members)], index)
            start = start + index * value.shape[0]
        return value, start

    def z_gather(value):
        for low, width in reversed(z_groups):
            members = 1 << width
            index = (aux >> low) & (members - 1)
            value = gather(value, [(s << low, 0) for s in range(members)], index)
        return value

    first = jnp.where(lane == 0, own, twin)
    second = jnp.where(lane == 0, twin, own)
    near = virt // 2
    left = lax.dynamic_slice_in_dim(first, lane * near, near, 1)
    side_ints = jnp.concatenate([tn(own, own), tn(left, second)], 0)
    x_flips = [(0, 0), (1, 0)]
    x_index = aux & 1
    part = scatter_sum(side_ints, x_flips, x_index)
    start = x_index * part.shape[0]
    part, more = z_scatter(part)
    start = start + more
    row = start + jnp.arange(part.shape[0])
    in_own = row < virt
    a_index = jnp.where(in_own, row, row - virt + lane * near)
    occ_i = jnp.where(in_own, pick(occ_side, lane), occ_side[0])
    occ_j = jnp.where(in_own, pick(occ_side, lane), occ_side[1])
    weight = jnp.where(
        in_own, mask[pair, pair], mask[2 * side, 2 * side + 1])
    row_term = jnp.take(vir_energy, a_index) - occ_i - occ_j
    part = weight[:, None] * part / (row_term[:, None] + vir_energy[None, :])
    side_amps = gather(z_gather(part), x_flips, x_index)
    own_amps = side_amps[:virt]
    mixed = side_amps[virt:]
    mixed_twin = across(mixed, 0, 1)
    mixed_amps = jnp.concatenate(
        [jnp.where(lane == 0, mixed, mixed_twin), jnp.where(lane == 0, mixed_twin, mixed)], 0)

    here = pick(pieces, side)
    twin_here = pick(twin.reshape(2, half, virt), side)
    facing_twin = across(facing_near, 0, 1)
    low = jnp.where(side == 0, here, facing_near)
    high = jnp.where(side == 0, facing_near, here)
    high_twin = jnp.where(side == 0, facing_twin, twin_here)
    high_first = jnp.where(lane == 0, high, high_twin)
    high_second = jnp.where(lane == 0, high_twin, high)
    cross_ints = jnp.concatenate([tn(low, high_first), tn(low, high_second)], 0)
    q_flips = [(0, 0), (1, 0), (0, 2), (1, 2)]
    q_index = (aux & 1) + 2 * side
    part = scatter_sum(cross_ints, q_flips, q_index)
    start = q_index * part.shape[0]
    part, more = z_scatter(part)
    start = start + more
    row = start + jnp.arange(part.shape[0])
    block = row // virt
    a_index = row % virt
    weight = jnp.where(block == 0, mask[lane, 2], mask[lane, 3])
    row_term = jnp.take(vir_energy, a_index) - pick(occ_low, lane) - jnp.where(
        block == 0, occ_high[0], occ_high[1])
    part = weight[:, None] * part / (row_term[:, None] + vir_energy[None, :])
    cross_amps = gather(z_gather(part), q_flips, q_index)

    cross_blocks = cross_amps.reshape(2, virt, virt)
    swapped = across(pick(cross_blocks, lane ^ 1), 0, 1)
    kept = pick(cross_blocks, lane)
    facing_far_twin = across(facing_far, 0, 1)
    zero_near = jnp.where(side == 0, facing_near, facing_far)
    zero_far = jnp.where(side == 0, facing_far, facing_near)
    facing = jnp.concatenate([zero_near, zero_far], 0)
    twin_near = jnp.where(side == 0, facing_twin, facing_far_twin)
    twin_far = jnp.where(side == 0, facing_far_twin, facing_twin)
    facing_t = jnp.concatenate([twin_near, twin_far], 0)
    f_first = jnp.where(lane == 0, facing, facing_t)
    f_second = jnp.where(lane == 0, facing_t, facing)
    low_amps = jnp.where(lane == 0, kept, swapped)
    high_amps = jnp.where(lane == 0, swapped, kept)
    m0 = jnp.where(side == 0, cross_blocks[0], low_amps.T)
    m1 = jnp.where(side == 0, cross_blocks[1], high_amps.T)
    mixed_use = jnp.where(lane == 0, mixed_amps, mixed_amps.T)
    gamma = nt(own, own_amps) + nt(twin, mixed_use) + nt(f_first, m0) + nt(f_second, m1)
    return gamma.reshape(rows, occ_count, virt)


def solution(mesh):
    in_specs = (P("aux", "pair", None), P("pair"), P(), P())
    out_specs = P("aux", "pair", None)
    return jax.shard_map(
        on_device, mesh=mesh, in_specs=in_specs, out_specs=out_specs, check_vma=False
    )
```

```python
import functools

import jax
import jax.numpy as jnp
from jax import lax
from jax.experimental import pallas as pl
from jax.experimental.pallas import tpu as pltpu
from jax.sharding import PartitionSpec as P

AXES = ("aux", "pair")
precision = lax.Precision.HIGH


def across(value, aux_flip, pair_flip):
    aux_count, pair_count = lax.axis_size("aux"), lax.axis_size("pair")
    moves = [
        (a * pair_count + p, (a ^ aux_flip) * pair_count + (p ^ pair_flip))
        for a in range(aux_count)
        for p in range(pair_count)
    ]
    return lax.ppermute(value, AXES, moves)


def pick(pieces, index):
    return lax.dynamic_index_in_dim(pieces, index, 0, keepdims=False)


def tn(left, right):
    return lax.dot_general(
        left, right, (((0,), (0,)), ((), ())), precision=precision,
        preferred_element_type=jnp.float32)


def nt(left, right):
    return lax.dot_general(
        left, right, (((1,), (1,)), ((), ())), precision=precision,
        preferred_element_type=jnp.float32)


def nn(left, right):
    return jnp.dot(left, right, precision=precision, preferred_element_type=jnp.float32)


def scatter_sum(value, flips, index):
    members = len(flips)
    pieces = value.reshape((members, value.shape[0] // members) + value.shape[1:])
    total = pick(pieces, index)
    for step in range(1, members):
        total = total + across(pick(pieces, index ^ step), *flips[step])
    return total


def gather(piece, flips, index):
    members = len(flips)
    whole = jnp.zeros((members,) + piece.shape, piece.dtype)
    whole = lax.dynamic_update_index_in_dim(whole, piece, index, 0)
    for step in range(1, members):
        whole = lax.dynamic_update_index_in_dim(
            whole, across(piece, *flips[step]), index ^ step, 0)
    return whole.reshape((members * piece.shape[0],) + piece.shape[1:])


def aux_groups(aux_count):
    bits = aux_count.bit_length() - 1
    low, groups = 1, []
    while low < bits:
        width = min(2, bits - low)
        groups.append((low, width))
        low += width
    return groups


def general_path(three_center, occ_energy, vir_energy, pair_mask):
    rows, occ_count, virt = three_center.shape
    aux_count = lax.axis_size("aux")
    aux, pair = lax.axis_index("aux"), lax.axis_index("pair")
    side, lane = pair // 2, pair % 2
    half = rows // 2
    own = three_center.reshape(rows, virt)
    pieces = own.reshape(2, half, virt)
    occ_side = jnp.stack([occ_energy[0], across(occ_energy, 0, 1)[0]])
    occ_side = jnp.where(lane == 0, occ_side, occ_side[::-1])
    occ_other = across(occ_side, 0, 2)
    occ_low = jnp.where(side == 0, occ_side, occ_other)
    occ_high = jnp.where(side == 0, occ_other, occ_side)
    mask = pair_mask.astype(jnp.float32)

    facing_near = across(pick(pieces, side ^ 1), 0, 2)
    twin = across(own, 0, 1)
    facing_far = across(pick(pieces, side), 0, 2)

    z_groups = aux_groups(aux_count)

    def z_scatter(value):
        start = jnp.int32(0)
        for low, width in z_groups:
            members = 1 << width
            index = (aux >> low) & (members - 1)
            value = scatter_sum(value, [(s << low, 0) for s in range(members)], index)
            start = start + index * value.shape[0]
        return value, start

    def z_gather(value):
        for low, width in reversed(z_groups):
            members = 1 << width
            index = (aux >> low) & (members - 1)
            value = gather(value, [(s << low, 0) for s in range(members)], index)
        return value

    first = jnp.where(lane == 0, own, twin)
    second = jnp.where(lane == 0, twin, own)
    near = virt // 2
    left = lax.dynamic_slice_in_dim(first, lane * near, near, 1)
    side_ints = jnp.concatenate([tn(own, own), tn(left, second)], 0)
    x_flips = [(0, 0), (1, 0)]
    x_index = aux & 1
    part = scatter_sum(side_ints, x_flips, x_index)
    start = x_index * part.shape[0]
    part, more = z_scatter(part)
    start = start + more
    row = start + jnp.arange(part.shape[0])
    in_own = row < virt
    a_index = jnp.where(in_own, row, row - virt + lane * near)
    occ_i = jnp.where(in_own, pick(occ_side, lane), occ_side[0])
    occ_j = jnp.where(in_own, pick(occ_side, lane), occ_side[1])
    weight = jnp.where(
        in_own, mask[pair, pair], mask[2 * side, 2 * side + 1])
    row_term = jnp.take(vir_energy, a_index) - occ_i - occ_j
    part = weight[:, None] * part / (row_term[:, None] + vir_energy[None, :])
    side_amps = gather(z_gather(part), x_flips, x_index)
    own_amps = side_amps[:virt]
    mixed = side_amps[virt:]
    mixed_twin = across(mixed, 0, 1)
    mixed_amps = jnp.concatenate(
        [jnp.where(lane == 0, mixed, mixed_twin), jnp.where(lane == 0, mixed_twin, mixed)], 0)

    here = pick(pieces, side)
    twin_here = pick(twin.reshape(2, half, virt), side)
    facing_twin = across(facing_near, 0, 1)
    low = jnp.where(side == 0, here, facing_near)
    high = jnp.where(side == 0, facing_near, here)
    high_twin = jnp.where(side == 0, facing_twin, twin_here)
    high_first = jnp.where(lane == 0, high, high_twin)
    high_second = jnp.where(lane == 0, high_twin, high)
    cross_ints = jnp.concatenate([tn(low, high_first), tn(low, high_second)], 0)
    q_flips = [(0, 0), (1, 0), (0, 2), (1, 2)]
    q_index = (aux & 1) + 2 * side
    part = scatter_sum(cross_ints, q_flips, q_index)
    start = q_index * part.shape[0]
    part, more = z_scatter(part)
    start = start + more
    row = start + jnp.arange(part.shape[0])
    block = row // virt
    a_index = row % virt
    weight = jnp.where(block == 0, mask[lane, 2], mask[lane, 3])
    row_term = jnp.take(vir_energy, a_index) - pick(occ_low, lane) - jnp.where(
        block == 0, occ_high[0], occ_high[1])
    part = weight[:, None] * part / (row_term[:, None] + vir_energy[None, :])
    cross_amps = gather(z_gather(part), q_flips, q_index)

    cross_blocks = cross_amps.reshape(2, virt, virt)
    swapped = across(pick(cross_blocks, lane ^ 1), 0, 1)
    kept = pick(cross_blocks, lane)
    facing_far_twin = across(facing_far, 0, 1)
    zero_near = jnp.where(side == 0, facing_near, facing_far)
    zero_far = jnp.where(side == 0, facing_far, facing_near)
    facing = jnp.concatenate([zero_near, zero_far], 0)
    twin_near = jnp.where(side == 0, facing_twin, facing_far_twin)
    twin_far = jnp.where(side == 0, facing_far_twin, facing_twin)
    facing_t = jnp.concatenate([twin_near, twin_far], 0)
    f_first = jnp.where(lane == 0, facing, facing_t)
    f_second = jnp.where(lane == 0, facing_t, facing)
    low_amps = jnp.where(lane == 0, kept, swapped)
    high_amps = jnp.where(lane == 0, swapped, kept)
    m0 = jnp.where(side == 0, cross_blocks[0], low_amps.T)
    m1 = jnp.where(side == 0, cross_blocks[1], high_amps.T)
    mixed_use = jnp.where(lane == 0, mixed_amps, mixed_amps.T)
    gamma = nt(own, own_amps) + nt(twin, mixed_use) + nt(f_first, m0) + nt(f_second, m1)
    return gamma.reshape(rows, occ_count, virt)


LANES = 128
IN_VMEM = pl.BlockSpec(memory_space=pltpu.VMEM)
IN_SMEM = pl.BlockSpec(memory_space=pltpu.SMEM)


def dot_tn(left, right):
    return lax.dot_general(
        left, right, (((0,), (0,)), ((), ())), preferred_element_type=jnp.float32)


def dot_nn(left, right):
    return jnp.dot(left, right, preferred_element_type=jnp.float32)


def halves(value):
    top = value.astype(jnp.bfloat16)
    return top, (value - top.astype(jnp.float32)).astype(jnp.bfloat16)


def spots():
    aux, pair = lax.axis_index("aux"), lax.axis_index("pair")
    return aux & 1, aux >> 1, pair >> 1, pair & 1, pair


def call(kernel, outs, args, in_smem=(), scratch=(), flops=0):
    moved = sum(a.size * 4 for a in args) + sum(4 * o[0] * o[1] for o in outs)
    result = pl.pallas_call(
        kernel,
        out_shape=[jax.ShapeDtypeStruct(o, jnp.float32) for o in outs],
        in_specs=[IN_SMEM if i in in_smem else IN_VMEM for i in range(len(args))],
        out_specs=[IN_VMEM for _ in outs],
        scratch_shapes=list(scratch),
        cost_estimate=pl.CostEstimate(flops=flops, bytes_accessed=moved, transcendentals=0),
    )(*args)
    return result


def unpack(ref, first_row, rows, chunks, top_ref, low_ref, slot):
    step = min(256, rows)

    @pl.loop(0, rows // step)
    def _(block):
        for c in range(chunks):
            start = (first_row + block * step) * chunks + c
            top, low = halves(ref[pl.ds(start, step, stride=chunks), :])
            where = pl.ds(pl.multiple_of(block * step, step), step)
            top_ref[slot, where, c * LANES:(c + 1) * LANES] = top
            low_ref[slot, where, c * LANES:(c + 1) * LANES] = low


def half_rows(top, low, left, right, lane, chunks, spare, store):
    full = chunks // 2

    def product(chunk):
        where = pl.ds(pl.multiple_of(chunk * LANES, LANES), LANES)
        lt, ll = top[left, :, where], low[left, :, where]
        rt, rl = top[right], low[right]
        return dot_tn(lt, rt) + (dot_tn(lt, rl) + dot_tn(ll, rt))

    for t in range(full):
        store(t * LANES, LANES, product(lane * (chunks - full) + t))
    if chunks % 2:
        spare[...] = product(full)
        part = LANES // 2
        store(full * LANES, part, spare[pl.ds(pl.multiple_of(lane * part, part), part), :])


def row_origin(row, lane, chunks):
    full = chunks // 2
    whole = full * LANES
    return jnp.where(
        row < whole, lane * (chunks - full) * LANES + row,
        full * LANES + lane * (LANES // 2) + row - whole)


def side_kernel(rows, chunks, own, twin, keep, send, top, low, acc, cross, spare):
    x, _, _, lane, _ = spots()
    virt = chunks * LANES
    unpack(own, 0, rows, chunks, top, low, lane)
    unpack(twin, 0, rows, chunks, top, low, 1 - lane)
    cross[...] = dot_tn(top[lane], low[lane])
    acc[0:virt, :] = dot_tn(top[lane], top[lane]) + (cross[...] + cross[...].T)

    def store(first, count, value):
        acc[virt + first:virt + first + count, :] = value

    half_rows(top, low, 0, 1, lane, chunks, spare, store)
    size = keep.shape[0]
    keep[...] = acc[pl.ds(pl.multiple_of(x * size, 8), size), :]
    send[...] = acc[pl.ds(pl.multiple_of((1 - x) * size, 8), size), :]


def side_pair(mask, slot, slots):
    if slots == 4:
        return slot // 2, 2 + slot % 2, mask[slot // 2, 2 + slot % 2]
    count, found, weight = jnp.int32(0), jnp.int32(0), jnp.int32(0)
    for k in range(4):
        live = mask[k // 2, 2 + k % 2]
        hit = (live > 0) & (count == slot)
        found = jnp.where(hit, k, found)
        weight = jnp.where(hit, live, weight)
        count = count + (live > 0).astype(jnp.int32)
    return found // 2, 2 + found % 2, weight


def cross_kernel(half, chunks, slots, mask, own, twin, face, face_twin, *rest):
    outs, (top, low, acc, spare) = rest[:4], rest[4:]
    x, _, side, lane, pair = spots()
    virt = chunks * LANES
    unpack(own, side * half, half, chunks, top, low, pair)
    unpack(twin, side * half, half, chunks, top, low, pair ^ 1)
    unpack(face, 0, half, chunks, top, low, pair ^ 2)
    unpack(face_twin, 0, half, chunks, top, low, pair ^ 3)
    for slot in range(slots):
        first, second, _ = side_pair(mask, slot, slots)

        def store(start, count, value, slot=slot):
            at = slot * virt // 2 + start
            acc[at:at + count, :] = value

        half_rows(top, low, first, second, lane, chunks, spare, store)
    size = outs[0].shape[0]
    square = x + 2 * side
    for step in range(4):
        outs[step][...] = acc[pl.ds(pl.multiple_of((square ^ step) * size, 8), size), :]


def add_kernel(members, *refs):
    _, z, _, _, _ = spots()
    ins, outs = refs[:members], refs[members:]
    count, size = len(outs), outs[0].shape[0]
    for step in range(count):
        where = pl.ds(pl.multiple_of((z ^ step) * size, 8), size)
        total = ins[0][where, :]
        for other in ins[1:]:
            total = total + other[where, :]
        outs[step][...] = total


def join_kernel(*refs):
    _, z, _, _, _ = spots()
    out, ins = refs[-1], refs[:-1]
    size = ins[0].shape[0]
    for step, piece in enumerate(ins):
        out[pl.ds(pl.multiple_of((z ^ step) * size, 8), size), :] = piece[...]


def scale_kernel(chunks, slots, members, mask, occ, vir_row, vir_col, *refs):
    x, z, side, lane, pair = spots()
    ins, out = refs[:members], refs[members]
    virt = chunks * LANES
    size = out.shape[0]
    start = ((x if slots == 0 else x + 2 * side) * members + z) * size
    for group in range(size // 8):
        row = start + group * 8
        if slots == 0:
            mixed = row >= virt
            first = jnp.where(mixed, 2 * side, pair)
            second = jnp.where(mixed, 2 * side + 1, pair)
            weight = mask[first, second]
            origin = jnp.where(mixed, row_origin(row - virt, lane, chunks), row)
        else:
            first, second, weight = side_pair(mask, 0, slots)
            for slot in range(1, slots):
                f, s, w = side_pair(mask, slot, slots)
                here = row >= slot * virt // 2
                first = jnp.where(here, f, first)
                second = jnp.where(here, s, second)
                weight = jnp.where(here, w, weight)
            origin = row_origin(row % (virt // 2), lane, chunks)
        here = slice(group * 8, group * 8 + 8)
        total = ins[0][here, :]
        for other in ins[1:]:
            total = total + other[here, :]
        energy = vir_col[pl.ds(pl.multiple_of(origin, 8), 8), :] + vir_row[...]
        energy = energy - occ[first] - occ[second]
        out[here, :] = weight.astype(jnp.float32) * total / energy


def place_block(halves_ref, first, chunks, whole):
    full = chunks // 2
    part = LANES // 2
    for lane in range(2):
        at = lane * (chunks - full) * LANES
        whole[at:at + full * LANES, :] = halves_ref[lane, pl.ds(first, full * LANES), :]
        if chunks % 2:
            at = full * LANES + lane * part
            whole[at:at + part, :] = halves_ref[
                lane, pl.ds(first + full * LANES, part), :]


def product3(flat, first_row, rows, chunks, stacked):
    parts = [
        halves(flat[pl.ds(first_row * chunks + c, rows, stride=chunks), :])
        for c in range(chunks)]
    tops, lows = [p[0] for p in parts], [p[1] for p in parts]
    return dot_nn(jnp.concatenate(tops + lows + tops, 1), stacked[...])


def stack(value, stacked):
    virt = value.shape[0]
    top, low = halves(value)
    stacked[0:virt, :] = top
    stacked[virt:2 * virt, :] = top
    stacked[2 * virt:3 * virt, :] = low


def near_gamma_kernel(rows, chunks, own, twin, keep, other, keep_t, other_t, out,
                      parts, whole, stacked):
    x, _, _, lane, _ = spots()
    virt = chunks * LANES
    size = keep.shape[0]
    for ref, slot, piece in ((keep, lane, x), (other, lane, 1 - x),
                             (keep_t, 1 - lane, x), (other_t, 1 - lane, 1 - x)):
        parts[slot, pl.ds(pl.multiple_of(piece * size, 8), size), :] = ref[...]
    stack(parts[lane, 0:virt, :], stacked.at[0])
    place_block(parts, virt, chunks, whole)

    @pl.when(lane == 0)
    def _():
        stack(whole[...].T, stacked.at[1])

    @pl.when(lane == 1)
    def _():
        stack(whole[...], stacked.at[1])

    step = min(256, rows)

    @pl.loop(0, rows // step)
    def _(block):
        at = block * step
        total = product3(own, at, step, chunks, stacked.at[0])
        total = total + product3(twin, at, step, chunks, stacked.at[1])
        out[pl.ds(pl.multiple_of(at, step), step), :] = total


def far_gamma_kernel(rows, chunks, slots, mask, base, near, far, near_t, far_t, *rest):
    pieces, pieces_t = rest[0:4], rest[4:8]
    out, parts, whole, stacked = rest[8:]
    x, _, side, lane, pair = spots()
    virt = chunks * LANES
    half = rows // 2
    size = pieces[0].shape[0]
    square = x + 2 * side
    for step in range(4):
        where = pl.ds(pl.multiple_of((square ^ step) * size, 8), size)
        parts[lane, where, :] = pieces[step][...]
        parts[1 - lane, where, :] = pieces_t[step][...]
    lives = []
    for flip in (0, 1):
        partner = pair ^ (2 + flip)
        first = jnp.minimum(pair, partner)
        second = jnp.maximum(pair, partner)
        live, at = jnp.int32(0), jnp.int32(0)
        for slot in range(slots):
            f, s, weight = side_pair(mask, slot, slots)
            hit = (f == first) & (s == second) & (weight > 0)
            live = jnp.where(hit, 1, live)
            at = jnp.where(hit, slot, at)
        place_block(parts, pl.multiple_of(at * (virt // 2), 8), chunks, whole)

        @pl.when(side == 0)
        def _(flip=flip):
            stack(whole[...].T, stacked.at[flip])

        @pl.when(side == 1)
        def _(flip=flip):
            stack(whole[...], stacked.at[flip])

        lives.append(live)
    step = min(256, half)
    for source, source_t, which in ((near, near_t, side), (far, far_t, 1 - side)):

        @pl.loop(0, half // step)
        def _(block, source=source, source_t=source_t, which=which):
            at = which * half + block * step
            total = base[pl.ds(pl.multiple_of(at, step), step), :]
            for flip, ref in ((0, source), (1, source_t)):
                total = lax.cond(
                    lives[flip] > 0,
                    lambda t, ref=ref, flip=flip: t + product3(
                        ref, block * step, step, chunks, stacked.at[flip]),
                    lambda t: t, total)
            for c in range(chunks):
                out[pl.ds(at * chunks + c, step, stride=chunks), :] = total[
                    :, c * LANES:(c + 1) * LANES]


def flat_kernel(rows, chunks, base, out):
    step = min(256, rows)

    @pl.loop(0, rows // step)
    def _(block):
        at = block * step
        for c in range(chunks):
            out[pl.ds(at * chunks + c, step, stride=chunks), :] = base[
                pl.ds(pl.multiple_of(at, step), step), c * LANES:(c + 1) * LANES]


def opening(three_center, occ_energy):
    rows, _, virt = three_center.shape
    chunks = virt // LANES
    half = rows // 2
    pair = lax.axis_index("pair")
    side, lane = pair // 2, pair % 2
    own = three_center.reshape(rows * chunks, LANES)
    flat_half = half * chunks
    bf16, f32 = jnp.bfloat16, jnp.float32
    near = across(pick(own.reshape(2, flat_half, LANES), 1 - side), 0, 2)
    twin = across(own, 0, 1)
    side_rows = virt + virt // 2
    keep, send = call(
        functools.partial(side_kernel, rows, chunks), [(side_rows // 2, virt)] * 2, [own, twin],
        scratch=[pltpu.VMEM((2, rows, virt), bf16)] * 2 + [
            pltpu.VMEM((side_rows, virt), f32), pltpu.VMEM((virt, virt), f32),
            pltpu.VMEM((LANES, virt), f32)], flops=12 * rows * virt * virt)
    got = across(send, 1, 0)
    occ_energy, got_first = lax.optimization_barrier((occ_energy, send))
    occ_side = jnp.concatenate([occ_energy, across(occ_energy, 0, 1)])
    occ_side = jnp.where(lane == 0, occ_side, occ_side[::-1])
    occ_other = across(occ_side, 0, 2)
    occ = jnp.where(side == 0, jnp.concatenate([occ_side, occ_other]),
                    jnp.concatenate([occ_other, occ_side]))
    near, keep, got, occ = lax.optimization_barrier((near, keep, got, occ))
    return own, twin, near, keep, got, occ


def closing(slots, shape, own, twin, near, keep, got, occ, vir_row, vir_col, pair_mask):
    rows, _, virt = shape
    chunks = virt // LANES
    half = rows // 2
    z_count = lax.axis_size("aux") // 2
    side = lax.axis_index("pair") // 2
    flat_half = half * chunks
    bf16, f32 = jnp.bfloat16, jnp.float32
    block_flops = 6 * rows * virt * virt
    energies = [pair_mask, occ, vir_row, vir_col]
    side_rows = virt + virt // 2
    piece_rows = side_rows // 2 // z_count
    total_rows = slots * virt // 2
    slab_rows = total_rows // 4 // z_count
    flips = [(0, 0), (1, 0), (0, 2), (1, 2)]

    def z_send(pieces):
        return [across(pieces[s], s << 1, 0) for s in range(1, z_count)]

    def z_spread(slab):
        return [slab] + [across(slab, s << 1, 0) for s in range(1, z_count)]

    if slots:
        near_t = across(near, 0, 1)
    pieces = call(functools.partial(add_kernel, 2), [(piece_rows, virt)] * z_count, [keep, got])
    if slots:
        near_t, pieces = lax.optimization_barrier((near_t, pieces))
        cross = call(
            functools.partial(cross_kernel, half, chunks, slots), [(total_rows // 4, virt)] * 4,
            [pair_mask, own, twin, near, near_t], in_smem=(0,),
            scratch=[pltpu.VMEM((4, half, virt), bf16)] * 2 + [
                pltpu.VMEM((total_rows, virt), f32), pltpu.VMEM((LANES, virt), f32)],
            flops=block_flops)
        cross, pieces = lax.optimization_barrier((cross, pieces))
        cross_got = [across(cross[s], *flips[s]) for s in range(1, 4)]
    side_got = z_send(pieces)
    if slots:
        pieces_c = call(functools.partial(add_kernel, 4), [(slab_rows, virt)] * z_count,
                        [cross[0], *cross_got])
        pieces_c, side_got = lax.optimization_barrier((pieces_c, side_got))
        z_got = z_send(pieces_c)
        far_send = pick(own.reshape(2, flat_half, LANES), side)
        far_send, pieces_c = lax.optimization_barrier((far_send, pieces_c))
        far = across(far_send, 0, 2)
    slab, = call(functools.partial(scale_kernel, chunks, 0, z_count), [(piece_rows, virt)],
                 [*energies, pieces[0], *side_got], in_smem=(0, 1))
    side_slabs = z_spread(slab)
    if slots:
        cross_slab, = call(
            functools.partial(scale_kernel, chunks, slots, z_count), [(slab_rows, virt)],
            [*energies, pieces_c[0], *z_got], in_smem=(0, 1))
        cross_slab, side_slabs = lax.optimization_barrier((cross_slab, side_slabs))
        cross_slabs = z_spread(cross_slab)
    joined, = call(join_kernel, [(side_rows // 2, virt)], side_slabs)
    other = across(joined, 1, 0)
    joined_t = across(joined, 0, 1)
    if slots:
        joined_c, = call(join_kernel, [(total_rows // 4, virt)], cross_slabs)
        joined_c, other, joined_t = lax.optimization_barrier((joined_c, other, joined_t))
        whole = [joined_c] + [across(joined_c, *flips[s]) for s in range(1, 4)]
        far_t = across(far, 0, 1)
    other_t = across(other, 0, 1)
    gamma, = call(
        functools.partial(near_gamma_kernel, rows, chunks), [(rows, virt)],
        [own, twin, joined, other, joined_t, other_t],
        scratch=[pltpu.VMEM((2, side_rows, virt), f32), pltpu.VMEM((virt, virt), f32),
                 pltpu.VMEM((2, 3 * virt, virt), bf16)], flops=2 * block_flops)
    if not slots:
        gamma, = call(functools.partial(flat_kernel, rows, chunks), [(rows * chunks, LANES)],
                      [gamma])
        return gamma
    whole_t = [across(piece, 0, 1) for piece in whole]
    gamma, = call(
        functools.partial(far_gamma_kernel, rows, chunks, slots), [(rows * chunks, LANES)],
        [pair_mask, gamma, near, far, near_t, far_t, *whole, *whole_t], in_smem=(0,),
        scratch=[pltpu.VMEM((2, total_rows, virt), f32), pltpu.VMEM((virt, virt), f32),
                 pltpu.VMEM((2, 3 * virt, virt), bf16)], flops=2 * block_flops)
    return gamma


def on_device(three_center, occ_energy, vir_energy, pair_mask):
    rows, occ_count, virt = three_center.shape
    aux_count, pair_count = lax.axis_size("aux"), lax.axis_size("pair")
    z_count = aux_count // 2
    fits = (
        occ_count == 1 and pair_count == 4 and z_count in (2, 4) and aux_count == 2 * z_count
        and virt % LANES == 0 and rows % 16 == 0
        and virt % (8 * z_count * 8 // 2) == 0 and (virt + virt // 2) % (16 * z_count) == 0)
    args = (three_center, occ_energy, vir_energy, pair_mask)
    if not fits:
        return general_path(*args)
    live = jnp.sum((pair_mask[:2, 2:] > 0).astype(jnp.int32))
    branch = (live > 0).astype(jnp.int32) + (live > 2).astype(jnp.int32)
    opened = opening(three_center, occ_energy)
    gamma = lax.switch(
        branch, [functools.partial(closing, n, three_center.shape) for n in BRANCHES],
        *opened, vir_energy.reshape(1, virt), vir_energy.reshape(virt, 1), pair_mask)
    return gamma.reshape(three_center.shape)


BRANCHES = (0, 2, 4)


def solution(mesh):
    in_specs = (P("aux", "pair", None), P("pair"), P(), P())
    out_specs = P("aux", "pair", None)
    return jax.shard_map(
        on_device, mesh=mesh, in_specs=in_specs, out_specs=out_specs, check_vma=False
    )
```

```python
import functools

import jax
import jax.numpy as jnp
from jax import lax
from jax.experimental import pallas as pl
from jax.experimental.pallas import tpu as pltpu
from jax.sharding import PartitionSpec as P

AXES = ("aux", "pair")
precision = lax.Precision.HIGH


def across(value, aux_flip, pair_flip):
    aux_count, pair_count = lax.axis_size("aux"), lax.axis_size("pair")
    moves = [
        (a * pair_count + p, (a ^ aux_flip) * pair_count + (p ^ pair_flip))
        for a in range(aux_count)
        for p in range(pair_count)
    ]
    return lax.ppermute(value, AXES, moves)


def pick(pieces, index):
    return lax.dynamic_index_in_dim(pieces, index, 0, keepdims=False)


def tn(left, right):
    return lax.dot_general(
        left, right, (((0,), (0,)), ((), ())), precision=precision,
        preferred_element_type=jnp.float32)


def nt(left, right):
    return lax.dot_general(
        left, right, (((1,), (1,)), ((), ())), precision=precision,
        preferred_element_type=jnp.float32)


def scatter_sum(value, flips, index):
    members = len(flips)
    pieces = value.reshape((members, value.shape[0] // members) + value.shape[1:])
    total = pick(pieces, index)
    for step in range(1, members):
        total = total + across(pick(pieces, index ^ step), *flips[step])
    return total


def gather(piece, flips, index):
    members = len(flips)
    whole = jnp.zeros((members,) + piece.shape, piece.dtype)
    whole = lax.dynamic_update_index_in_dim(whole, piece, index, 0)
    for step in range(1, members):
        whole = lax.dynamic_update_index_in_dim(
            whole, across(piece, *flips[step]), index ^ step, 0)
    return whole.reshape((members * piece.shape[0],) + piece.shape[1:])


def aux_groups(aux_count):
    bits = aux_count.bit_length() - 1
    low, groups = 1, []
    while low < bits:
        width = min(2, bits - low)
        groups.append((low, width))
        low += width
    return groups


def general_path(three_center, occ_energy, vir_energy, pair_mask):
    rows, occ_count, virt = three_center.shape
    aux_count = lax.axis_size("aux")
    aux, pair = lax.axis_index("aux"), lax.axis_index("pair")
    side, lane = pair // 2, pair % 2
    half = rows // 2
    own = three_center.reshape(rows, virt)
    pieces = own.reshape(2, half, virt)
    occ_side = jnp.stack([occ_energy[0], across(occ_energy, 0, 1)[0]])
    occ_side = jnp.where(lane == 0, occ_side, occ_side[::-1])
    occ_other = across(occ_side, 0, 2)
    occ_low = jnp.where(side == 0, occ_side, occ_other)
    occ_high = jnp.where(side == 0, occ_other, occ_side)
    mask = pair_mask.astype(jnp.float32)

    facing_near = across(pick(pieces, side ^ 1), 0, 2)
    twin = across(own, 0, 1)
    facing_far = across(pick(pieces, side), 0, 2)

    z_groups = aux_groups(aux_count)

    def z_scatter(value):
        start = jnp.int32(0)
        for low, width in z_groups:
            members = 1 << width
            index = (aux >> low) & (members - 1)
            value = scatter_sum(value, [(s << low, 0) for s in range(members)], index)
            start = start + index * value.shape[0]
        return value, start

    def z_gather(value):
        for low, width in reversed(z_groups):
            members = 1 << width
            index = (aux >> low) & (members - 1)
            value = gather(value, [(s << low, 0) for s in range(members)], index)
        return value

    first = jnp.where(lane == 0, own, twin)
    second = jnp.where(lane == 0, twin, own)
    near = virt // 2
    left = lax.dynamic_slice_in_dim(first, lane * near, near, 1)
    side_ints = jnp.concatenate([tn(own, own), tn(left, second)], 0)
    x_flips = [(0, 0), (1, 0)]
    x_index = aux & 1
    part = scatter_sum(side_ints, x_flips, x_index)
    start = x_index * part.shape[0]
    part, more = z_scatter(part)
    start = start + more
    row = start + jnp.arange(part.shape[0])
    in_own = row < virt
    a_index = jnp.where(in_own, row, row - virt + lane * near)
    occ_i = jnp.where(in_own, pick(occ_side, lane), occ_side[0])
    occ_j = jnp.where(in_own, pick(occ_side, lane), occ_side[1])
    weight = jnp.where(
        in_own, mask[pair, pair], mask[2 * side, 2 * side + 1])
    row_term = jnp.take(vir_energy, a_index) - occ_i - occ_j
    part = weight[:, None] * part / (row_term[:, None] + vir_energy[None, :])
    side_amps = gather(z_gather(part), x_flips, x_index)
    own_amps = side_amps[:virt]
    mixed = side_amps[virt:]
    mixed_twin = across(mixed, 0, 1)
    mixed_amps = jnp.concatenate(
        [jnp.where(lane == 0, mixed, mixed_twin), jnp.where(lane == 0, mixed_twin, mixed)], 0)

    here = pick(pieces, side)
    twin_here = pick(twin.reshape(2, half, virt), side)
    facing_twin = across(facing_near, 0, 1)
    low = jnp.where(side == 0, here, facing_near)
    high = jnp.where(side == 0, facing_near, here)
    high_twin = jnp.where(side == 0, facing_twin, twin_here)
    high_first = jnp.where(lane == 0, high, high_twin)
    high_second = jnp.where(lane == 0, high_twin, high)
    cross_ints = jnp.concatenate([tn(low, high_first), tn(low, high_second)], 0)
    q_flips = [(0, 0), (1, 0), (0, 2), (1, 2)]
    q_index = (aux & 1) + 2 * side
    part = scatter_sum(cross_ints, q_flips, q_index)
    start = q_index * part.shape[0]
    part, more = z_scatter(part)
    start = start + more
    row = start + jnp.arange(part.shape[0])
    block = row // virt
    a_index = row % virt
    weight = jnp.where(block == 0, mask[lane, 2], mask[lane, 3])
    row_term = jnp.take(vir_energy, a_index) - pick(occ_low, lane) - jnp.where(
        block == 0, occ_high[0], occ_high[1])
    part = weight[:, None] * part / (row_term[:, None] + vir_energy[None, :])
    cross_amps = gather(z_gather(part), q_flips, q_index)

    cross_blocks = cross_amps.reshape(2, virt, virt)
    swapped = across(pick(cross_blocks, lane ^ 1), 0, 1)
    kept = pick(cross_blocks, lane)
    facing_far_twin = across(facing_far, 0, 1)
    zero_near = jnp.where(side == 0, facing_near, facing_far)
    zero_far = jnp.where(side == 0, facing_far, facing_near)
    facing = jnp.concatenate([zero_near, zero_far], 0)
    twin_near = jnp.where(side == 0, facing_twin, facing_far_twin)
    twin_far = jnp.where(side == 0, facing_far_twin, facing_twin)
    facing_t = jnp.concatenate([twin_near, twin_far], 0)
    f_first = jnp.where(lane == 0, facing, facing_t)
    f_second = jnp.where(lane == 0, facing_t, facing)
    low_amps = jnp.where(lane == 0, kept, swapped)
    high_amps = jnp.where(lane == 0, swapped, kept)
    m0 = jnp.where(side == 0, cross_blocks[0], low_amps.T)
    m1 = jnp.where(side == 0, cross_blocks[1], high_amps.T)
    mixed_use = jnp.where(lane == 0, mixed_amps, mixed_amps.T)
    gamma = nt(own, own_amps) + nt(twin, mixed_use) + nt(f_first, m0) + nt(f_second, m1)
    return gamma.reshape(rows, occ_count, virt)


LANES = 128
IN_VMEM = pl.BlockSpec(memory_space=pltpu.VMEM)
IN_SMEM = pl.BlockSpec(memory_space=pltpu.SMEM)
SLOTS = (1, 2, 4)
WHOLE_SLOTS = 2
STEP = 512


def dot_tn(left, right):
    return lax.dot_general(
        left, right, (((0,), (0,)), ((), ())), preferred_element_type=jnp.float32)


def dot_nn(left, right):
    return jnp.dot(left, right, preferred_element_type=jnp.float32)


def halves(value):
    top = value.astype(jnp.bfloat16)
    return top, (value - top.astype(jnp.float32)).astype(jnp.bfloat16)


def spots():
    aux, pair = lax.axis_index("aux"), lax.axis_index("pair")
    return aux & 1, aux >> 1, pair >> 1, pair & 1, pair


def call(kernel, outs, args, in_smem=(), scratch=(), flops=0):
    outs = [jax.ShapeDtypeStruct(o[:2], o[2] if len(o) > 2 else jnp.float32) for o in outs]
    moved = sum(a.size * a.dtype.itemsize for a in (*args, *outs))
    return pl.pallas_call(
        kernel,
        out_shape=outs,
        in_specs=[IN_SMEM if i in in_smem else IN_VMEM for i in range(len(args))],
        out_specs=[IN_VMEM for _ in outs],
        scratch_shapes=list(scratch),
        cost_estimate=pl.CostEstimate(flops=flops, bytes_accessed=moved, transcendentals=0),
    )(*args)


def unpack(ref, rows, chunks, top_ref, low_ref):
    step = min(256, rows)

    @pl.loop(0, rows // step)
    def _(block):
        for c in range(chunks):
            top, low = halves(ref[pl.ds(block * step * chunks + c, step, stride=chunks), :])
            where = pl.ds(pl.multiple_of(block * step, step), step)
            top_ref[where, c * LANES:(c + 1) * LANES] = top
            low_ref[where, c * LANES:(c + 1) * LANES] = low


def half_rows(left, right, lane, chunks, spare, store):
    full = chunks // 2

    def product(chunk):
        where = pl.ds(pl.multiple_of(chunk * LANES, LANES), LANES)
        lt, ll = left[0][:, where], left[1][:, where]
        rt, rl = right[0][...], right[1][...]
        return dot_tn(lt, rt) + (dot_tn(lt, rl) + dot_tn(ll, rt))

    for t in range(full):
        store(t * LANES, LANES, product(lane * (chunks - full) + t))
    if chunks % 2:
        spare[...] = product(full)
        part = LANES // 2
        store(full * LANES, part, spare[pl.ds(pl.multiple_of(lane * part, part), part), :])


def row_origin(row, lane, chunks):
    full = chunks // 2
    whole = full * LANES
    return jnp.where(
        row < whole, lane * (chunks - full) * LANES + row,
        full * LANES + lane * (LANES // 2) + row - whole)


def own_kernel(rows, chunks, own, keep, send, top, low, acc, cross):
    x, _, _, _, _ = spots()
    unpack(own, rows, chunks, top, low)
    cross[...] = dot_tn(top[...], low[...])
    acc[...] = dot_tn(top[...], top[...]) + (cross[...] + cross[...].T)
    size = keep.shape[0]
    keep[...] = acc[pl.ds(pl.multiple_of(x * size, 8), size), :]
    send[...] = acc[pl.ds(pl.multiple_of((1 - x) * size, 8), size), :]


def twin_kernel(rows, chunks, own_top, own_low, twin, keep, send, top, low, acc, spare):
    x, _, _, lane, _ = spots()
    unpack(twin, rows, chunks, top, low)

    def store(first, count, value):
        acc[first:first + count, :] = value

    own, other = (own_top, own_low), (top, low)
    for here, left, right in ((0, own, other), (1, other, own)):

        @pl.when(lane == here)
        def _(here=here, left=left, right=right):
            half_rows(left, right, here, chunks, spare, store)

    size = keep.shape[0]
    keep[...] = acc[pl.ds(pl.multiple_of(x * size, 8), size), :]
    send[...] = acc[pl.ds(pl.multiple_of((1 - x) * size, 8), size), :]


def side_pair(mask, slot, slots):
    if slots == 4:
        return slot // 2, 2 + slot % 2, mask[slot // 2, 2 + slot % 2]
    count, found, weight = jnp.int32(0), jnp.int32(0), jnp.int32(0)
    for k in range(4):
        live = mask[k // 2, 2 + k % 2]
        hit = (live > 0) & (count == slot)
        found = jnp.where(hit, k, found)
        weight = jnp.where(hit, live, weight)
        count = count + (live > 0).astype(jnp.int32)
    return found // 2, 2 + found % 2, weight


def cross_kernel(half, chunks, mask, own_top, own_low, twin_top, twin_low, face, face_twin,
                 *rest):
    outs, (face_tops, face_lows), (top, low, acc, spare) = rest[:-6], rest[-6:-4], rest[-4:]
    x, _, side, lane, pair = spots()
    virt = chunks * LANES
    rows = pl.ds(pl.multiple_of(side * half, half), half)
    top[pair], low[pair] = own_top[rows, :], own_low[rows, :]
    top[pair ^ 1], low[pair ^ 1] = twin_top[rows, :], twin_low[rows, :]
    for ref, flip in ((face, 2), (face_twin, 3)):
        which = pair ^ flip
        unpack(ref, half, chunks, top.at[which], low.at[which])
        at = slice((flip - 2) * half, (flip - 1) * half)
        face_tops[at, :], face_lows[at, :] = top[which], low[which]
    live = jnp.int32(0)
    for k in range(4):
        live = live + (mask[k // 2, 2 + k % 2] > 0).astype(jnp.int32)
    square = x + 2 * side
    for number, slots in enumerate(SLOTS):
        fewer = SLOTS[number - 1] if number else 0

        @pl.when((live > fewer) & (live <= slots))
        def _(number=number, slots=slots):
            for slot in range(slots):
                first, second, _ = side_pair(mask, slot, slots)

                def store(start, count, value, slot=slot):
                    at = slot * virt // 2 + start
                    acc[at:at + count, :] = value

                half_rows((top.at[first], low.at[first]), (top.at[second], low.at[second]),
                          lane, chunks, spare, store)
            mine = outs[4 * number:4 * number + 4]
            size = mine[0].shape[0]
            for step in range(4):
                mine[step][...] = acc[
                    pl.ds(pl.multiple_of((square ^ step) * size, 8), size), :]


def add_kernel(members, sets, *refs):
    _, z, _, _, _ = spots()
    ins, outs = refs[:members * sets], refs[members * sets:]
    count = len(outs)
    at = 0
    for which in range(sets):
        mine = ins[which * members:(which + 1) * members]
        size = mine[0].shape[0] // count
        for step in range(count):
            where = pl.ds(pl.multiple_of((z ^ step) * size, 8), size)
            total = mine[0][where, :]
            for other in mine[1:]:
                total = total + other[where, :]
            outs[step][at:at + size, :] = total
        at += size


def sum_kernel(*refs):
    total = refs[0][...]
    for other in refs[1:-1]:
        total = total + other[...]
    refs[-1][...] = total


def join_kernel(sizes, *refs):
    _, z, _, _, _ = spots()
    out, ins = refs[-1], refs[:-1]
    inner = outer = 0
    for size in sizes:
        for step, piece in enumerate(ins):
            at = pl.multiple_of(outer + (z ^ step) * size, 8)
            out[pl.ds(at, size), :] = piece[inner:inner + size, :]
        inner += size
        outer += size * len(ins)


def scale_kernel(chunks, slots, members, cut, mask, occ, vir_row, vir_col, *refs):
    x, z, side, lane, pair = spots()
    ins, out = refs[:members], refs[members]
    virt = chunks * LANES
    size = out.shape[0]
    own_size = size * 2 // 3
    for group in range(size // 8):
        row = group * 8
        if slots == 0:
            mixed = row >= own_size
            if mixed:
                row = (x * members + z) * (size - own_size) + row - own_size
                first, second = 2 * side, 2 * side + 1
                origin = row_origin(row, lane, chunks)
            else:
                origin = (x * members + z) * own_size + row
                first = second = pair
            weight = mask[first, second]
        else:
            row = ((x + 2 * side) * (members if cut else 1) + (z if cut else 0)) * size + row
            first, second, weight = side_pair(mask, 0, slots)
            for slot in range(1, slots):
                f, s, w = side_pair(mask, slot, slots)
                here = row >= slot * virt // 2
                first = jnp.where(here, f, first)
                second = jnp.where(here, s, second)
                weight = jnp.where(here, w, weight)
            origin = row_origin(row % (virt // 2), lane, chunks)
        here = slice(group * 8, group * 8 + 8)
        total = ins[0][here, :]
        for other in ins[1:]:
            total = total + other[here, :]
        energy = vir_col[pl.ds(pl.multiple_of(origin, 8), 8), :] + vir_row[...]
        energy = energy - occ[first] - occ[second]
        out[here, :] = weight.astype(jnp.float32) * total / energy


def place_block(halves_ref, first, chunks, whole):
    full = chunks // 2
    part = LANES // 2
    for lane in range(2):
        at = lane * (chunks - full) * LANES
        whole[at:at + full * LANES, :] = halves_ref[lane, pl.ds(first, full * LANES), :]
        if chunks % 2:
            at = full * LANES + lane * part
            whole[at:at + part, :] = halves_ref[
                lane, pl.ds(first + full * LANES, part), :]


def wide(top, low):
    return jnp.concatenate([top, low, top], 1)


def stack(value, stacked):
    virt = value.shape[0]
    top, low = halves(value)
    stacked[0:virt, :] = top
    stacked[virt:2 * virt, :] = top
    stacked[2 * virt:3 * virt, :] = low


def near_gamma_kernel(rows, chunks, own_top, own_low, twin_top, twin_low,
                      keep, other, keep_t, other_t, out, parts, whole, stacked):
    x, _, _, lane, _ = spots()
    virt = chunks * LANES
    size = keep.shape[0]
    own_size = size * 2 // 3
    mixed = size - own_size
    for ref, slot, piece in ((keep, lane, x), (other, lane, 1 - x),
                             (keep_t, 1 - lane, x), (other_t, 1 - lane, 1 - x)):
        parts[slot, pl.ds(pl.multiple_of(piece * own_size, 8), own_size), :] = ref[:own_size, :]
        parts[slot, pl.ds(pl.multiple_of(virt + piece * mixed, 8), mixed), :] = ref[own_size:, :]
    stack(parts[lane, 0:virt, :], stacked.at[0])
    place_block(parts, virt, chunks, whole)

    @pl.when(lane == 0)
    def _():
        stack(whole[...].T, stacked.at[1])

    @pl.when(lane == 1)
    def _():
        stack(whole[...], stacked.at[1])

    step = min(STEP, rows)

    @pl.loop(0, rows // step)
    def _(block):
        at = pl.ds(pl.multiple_of(block * step, step), step)
        out[at, :] = dot_nn(wide(own_top[at, :], own_low[at, :]), stacked[0]) + dot_nn(
            wide(twin_top[at, :], twin_low[at, :]), stacked[1])


def far_gamma_kernel(rows, chunks, slots, mask, base, face_tops, face_lows, far, far_t, *rest):
    pieces, pieces_t = rest[0:4], rest[4:8]
    out, parts, whole, stacked, total = rest[8:]
    x, _, side, lane, pair = spots()
    virt = chunks * LANES
    half = rows // 2
    size = pieces[0].shape[0]
    square = x + 2 * side
    for step in range(4):
        where = pl.ds(pl.multiple_of((square ^ step) * size, 8), size)
        parts[lane, where, :] = pieces[step][...]
        parts[1 - lane, where, :] = pieces_t[step][...]
    step = min(STEP, half)
    total[...] = base[...]
    for flip in (0, 1):
        partner = pair ^ (2 + flip)
        first = jnp.minimum(pair, partner)
        second = jnp.maximum(pair, partner)
        live, at = jnp.int32(0), jnp.int32(0)
        for slot in range(slots):
            f, s, weight = side_pair(mask, slot, slots)
            hit = (f == first) & (s == second) & (weight > 0)
            live = jnp.where(hit, 1, live)
            at = jnp.where(hit, slot, at)

        @pl.when(live > 0)
        def _(flip=flip, at=at):
            place_block(parts, pl.multiple_of(at * (virt // 2), 8), chunks, whole)

            @pl.when(side == 0)
            def _():
                stack(whole[...].T, stacked)

            @pl.when(side == 1)
            def _():
                stack(whole[...], stacked)

            @pl.loop(0, half // step)
            def _(block):
                rows_in = pl.ds(pl.multiple_of(flip * half + block * step, step), step)
                rows_out = pl.ds(pl.multiple_of(side * half + block * step, step), step)
                total[rows_out, :] += dot_nn(
                    wide(face_tops[rows_in, :], face_lows[rows_in, :]), stacked[...])
                source = far_t if flip else far
                parts_in = [
                    halves(source[pl.ds(block * step * chunks + c, step, stride=chunks), :])
                    for c in range(chunks)]
                tops, lows = [p[0] for p in parts_in], [p[1] for p in parts_in]
                rows_out = pl.ds(pl.multiple_of((1 - side) * half + block * step, step), step)
                total[rows_out, :] += dot_nn(
                    jnp.concatenate(tops + lows + tops, 1), stacked[...])

    flat_kernel(rows, chunks, total, out)


def flat_kernel(rows, chunks, base, out):
    step = min(256, rows)

    @pl.loop(0, rows // step)
    def _(block):
        at = block * step
        for c in range(chunks):
            out[pl.ds(at * chunks + c, step, stride=chunks), :] = base[
                pl.ds(pl.multiple_of(at, step), step), c * LANES:(c + 1) * LANES]


def opening(three_center, occ_energy, pair_mask):
    rows, _, virt = three_center.shape
    chunks = virt // LANES
    half = rows // 2
    z_count = lax.axis_size("aux") // 2
    pair = lax.axis_index("pair")
    side, lane = pair // 2, pair % 2
    own = three_center.reshape(rows * chunks, LANES)
    bf16, f32 = jnp.bfloat16, jnp.float32
    block_flops = 6 * rows * virt * virt
    flat_pieces = own.reshape(2, half * chunks, LANES)
    near = across(pick(flat_pieces, 1 - side), 0, 2)
    twin = across(own, 0, 1)
    split = [(rows, virt, bf16)] * 2
    mixed_rows = virt // 2
    occ_side = jnp.concatenate([occ_energy, across(occ_energy, 0, 1)])
    occ_side = jnp.where(lane == 0, occ_side, occ_side[::-1])
    occ_other = across(occ_side, 0, 2)
    occ = jnp.where(side == 0, jnp.concatenate([occ_side, occ_other]),
                    jnp.concatenate([occ_other, occ_side]))
    keep_a, send_a, own_top, own_low = call(
        functools.partial(own_kernel, rows, chunks), [(virt // 2, virt)] * 2 + split, [own],
        scratch=[pltpu.VMEM((virt, virt), f32)] * 2, flops=block_flops)
    got_a = across(send_a, 1, 0)
    twin, send_a = lax.optimization_barrier((twin, send_a))
    keep_b, send_b, twin_top, twin_low = call(
        functools.partial(twin_kernel, rows, chunks), [(mixed_rows // 2, virt)] * 2 + split,
        [own_top, own_low, twin],
        scratch=[pltpu.VMEM((mixed_rows, virt), f32), pltpu.VMEM((LANES, virt), f32)],
        flops=block_flops)
    got_b = across(send_b, 1, 0)
    piece_rows = (virt + mixed_rows) // 2 // z_count
    pieces = call(functools.partial(add_kernel, 2, 2), [(piece_rows, virt)] * z_count,
                   [keep_a, got_a, keep_b, got_b])
    side_got = [across(pieces[s], s << 1, 0) for s in range(1, z_count)]
    near_t = across(near, 0, 1)
    most = SLOTS[-1] * mixed_rows
    cross = call(
        functools.partial(cross_kernel, half, chunks),
        [(n * mixed_rows // 4, virt) for n in SLOTS for _ in range(4)] + split,
        [pair_mask, own_top, own_low, twin_top, twin_low, near, near_t], in_smem=(0,),
        scratch=[pltpu.VMEM((4, half, virt), bf16)] * 2 + [
            pltpu.VMEM((most, virt), f32), pltpu.VMEM((LANES, virt), f32)],
        flops=block_flops)
    cross, faces = cross[:-2], cross[-2:]
    far_send = pick(flat_pieces, side)
    return lax.optimization_barrier((
        (own_top, own_low, twin_top, twin_low), faces, far_send, occ,
        [pieces[0], *side_got], cross))


def closing(slots, shape, opened, vir_row, vir_col, pair_mask):
    splits, faces, far_send, occ, side_parts, cross = opened
    rows, _, virt = shape
    chunks = virt // LANES
    z_count = lax.axis_size("aux") // 2
    bf16, f32 = jnp.bfloat16, jnp.float32
    block_flops = 6 * rows * virt * virt
    energies = [pair_mask, occ, vir_row, vir_col]
    piece_rows = side_parts[0].shape[0]
    own_size = piece_rows * 2 // 3
    total_rows = slots * virt // 2
    square_rows = total_rows // 4
    slab_rows = square_rows // z_count
    flips = [(0, 0), (1, 0), (0, 2), (1, 2)]

    def z_spread(slab):
        return [across(slab, s << 1, 0) for s in range(1, z_count)]

    if slots:
        at = 4 * SLOTS.index(slots)
        cross = cross[at:at + 4]
        cross_got = [across(cross[s], *flips[s]) for s in range(1, 4)]
    slab, = call(
        functools.partial(scale_kernel, chunks, 0, z_count, True),
        [(piece_rows, virt)], [*energies, *side_parts], in_smem=(0, 1))
    side_slabs = [slab] + z_spread(slab)
    joined, = call(
        functools.partial(join_kernel, (own_size, piece_rows - own_size)),
        [(piece_rows * z_count, virt)], side_slabs)
    other = across(joined, 1, 0)
    joined_t = across(joined, 0, 1)
    other_t = across(other, 0, 1)
    gamma, = call(
        functools.partial(near_gamma_kernel, rows, chunks), [(rows, virt)],
        [*splits, joined, other, joined_t, other_t],
        scratch=[pltpu.VMEM((2, virt + virt // 2, virt), f32), pltpu.VMEM((virt, virt), f32),
                 pltpu.VMEM((2, 3 * virt, virt), bf16)], flops=2 * block_flops)
    if not slots:
        gamma, = call(functools.partial(flat_kernel, rows, chunks), [(rows * chunks, LANES)],
                      [gamma])
        return gamma
    if slots <= WHOLE_SLOTS:
        summed, = call(sum_kernel, [(square_rows, virt)], [cross[0], *cross_got])
        z_got = z_spread(summed)
        joined_c, = call(
            functools.partial(scale_kernel, chunks, slots, z_count, False),
            [(square_rows, virt)], [*energies, summed, *z_got], in_smem=(0, 1))
    else:
        pieces_c = call(
            functools.partial(add_kernel, 4, 1), [(slab_rows, virt)] * z_count,
            [cross[0], *cross_got])
        summed = pieces_c[0]
        z_got = [across(pieces_c[s], s << 1, 0) for s in range(1, z_count)]
        cross_slab, = call(
            functools.partial(scale_kernel, chunks, slots, z_count, True),
            [(slab_rows, virt)], [*energies, pieces_c[0], *z_got], in_smem=(0, 1))
        joined_c, = call(
            functools.partial(join_kernel, (slab_rows,)), [(square_rows, virt)],
            [cross_slab] + z_spread(cross_slab))
    far_send, summed = lax.optimization_barrier((far_send, summed))
    far = across(far_send, 0, 2)
    far_t = across(far, 0, 1)
    whole = [across(joined_c, *flips[s]) for s in range(1, 4)]
    joined_ct = across(joined_c, 0, 1)
    whole_t = [across(piece, 0, 1) for piece in whole]
    gamma, = call(
        functools.partial(far_gamma_kernel, rows, chunks, slots),
        [(rows * chunks, LANES)],
        [pair_mask, gamma, *faces, far, far_t, joined_c, *whole, joined_ct, *whole_t],
        in_smem=(0,),
        scratch=[pltpu.VMEM((2, total_rows, virt), f32), pltpu.VMEM((virt, virt), f32),
                 pltpu.VMEM((3 * virt, virt), bf16), pltpu.VMEM((rows, virt), f32)],
        flops=2 * block_flops)
    return gamma


def on_device(three_center, occ_energy, vir_energy, pair_mask):
    rows, occ_count, virt = three_center.shape
    aux_count, pair_count = lax.axis_size("aux"), lax.axis_size("pair")
    z_count = aux_count // 2
    fits = (
        occ_count == 1 and pair_count == 4 and z_count in (2, 4) and aux_count == 2 * z_count
        and virt % LANES == 0 and rows % 16 == 0
        and virt % (8 * z_count * 8 // 2) == 0 and (virt + virt // 2) % (16 * z_count) == 0)
    args = (three_center, occ_energy, vir_energy, pair_mask)
    if not fits:
        return general_path(*args)
    live = jnp.sum((pair_mask[:2, 2:] > 0).astype(jnp.int32))
    branch = jnp.int32(0)
    for slots in (0, *SLOTS[:-1]):
        branch = branch + (live > slots).astype(jnp.int32)
    opened = opening(three_center, occ_energy, pair_mask)
    gamma = lax.switch(
        branch, [functools.partial(closing, n, three_center.shape)
                 for n in (0, *SLOTS)],
        opened, vir_energy.reshape(1, virt), vir_energy.reshape(virt, 1), pair_mask)
    return gamma.reshape(three_center.shape)


def solution(mesh):
    in_specs = (P("aux", "pair", None), P("pair"), P(), P())
    out_specs = P("aux", "pair", None)
    return jax.shard_map(
        on_device, mesh=mesh, in_specs=in_specs, out_specs=out_specs, check_vma=False
    )
```

```python
import functools

import jax
import jax.numpy as jnp
from jax import lax
from jax.experimental import pallas as pl
from jax.experimental.pallas import tpu as pltpu
from jax.sharding import PartitionSpec as P

AXES = ("aux", "pair")
precision = lax.Precision.HIGH


def across(value, aux_flip, pair_flip):
    aux_count, pair_count = lax.axis_size("aux"), lax.axis_size("pair")
    moves = [
        (a * pair_count + p, (a ^ aux_flip) * pair_count + (p ^ pair_flip))
        for a in range(aux_count)
        for p in range(pair_count)
    ]
    return lax.ppermute(value, AXES, moves)


def pick(pieces, index):
    return lax.dynamic_index_in_dim(pieces, index, 0, keepdims=False)


def tn(left, right):
    return lax.dot_general(
        left, right, (((0,), (0,)), ((), ())), precision=precision,
        preferred_element_type=jnp.float32)


def nt(left, right):
    return lax.dot_general(
        left, right, (((1,), (1,)), ((), ())), precision=precision,
        preferred_element_type=jnp.float32)


def scatter_sum(value, flips, index):
    members = len(flips)
    pieces = value.reshape((members, value.shape[0] // members) + value.shape[1:])
    total = pick(pieces, index)
    for step in range(1, members):
        total = total + across(pick(pieces, index ^ step), *flips[step])
    return total


def gather(piece, flips, index):
    members = len(flips)
    whole = jnp.zeros((members,) + piece.shape, piece.dtype)
    whole = lax.dynamic_update_index_in_dim(whole, piece, index, 0)
    for step in range(1, members):
        whole = lax.dynamic_update_index_in_dim(
            whole, across(piece, *flips[step]), index ^ step, 0)
    return whole.reshape((members * piece.shape[0],) + piece.shape[1:])


def aux_groups(aux_count):
    bits = aux_count.bit_length() - 1
    low, groups = 1, []
    while low < bits:
        width = min(2, bits - low)
        groups.append((low, width))
        low += width
    return groups


def general_path(three_center, occ_energy, vir_energy, pair_mask):
    rows, occ_count, virt = three_center.shape
    aux_count = lax.axis_size("aux")
    aux, pair = lax.axis_index("aux"), lax.axis_index("pair")
    side, lane = pair // 2, pair % 2
    half = rows // 2
    own = three_center.reshape(rows, virt)
    pieces = own.reshape(2, half, virt)
    occ_side = jnp.stack([occ_energy[0], across(occ_energy, 0, 1)[0]])
    occ_side = jnp.where(lane == 0, occ_side, occ_side[::-1])
    occ_other = across(occ_side, 0, 2)
    occ_low = jnp.where(side == 0, occ_side, occ_other)
    occ_high = jnp.where(side == 0, occ_other, occ_side)
    mask = pair_mask.astype(jnp.float32)

    facing_near = across(pick(pieces, side ^ 1), 0, 2)
    twin = across(own, 0, 1)
    facing_far = across(pick(pieces, side), 0, 2)

    z_groups = aux_groups(aux_count)

    def z_scatter(value):
        start = jnp.int32(0)
        for low, width in z_groups:
            members = 1 << width
            index = (aux >> low) & (members - 1)
            value = scatter_sum(value, [(s << low, 0) for s in range(members)], index)
            start = start + index * value.shape[0]
        return value, start

    def z_gather(value):
        for low, width in reversed(z_groups):
            members = 1 << width
            index = (aux >> low) & (members - 1)
            value = gather(value, [(s << low, 0) for s in range(members)], index)
        return value

    first = jnp.where(lane == 0, own, twin)
    second = jnp.where(lane == 0, twin, own)
    near = virt // 2
    left = lax.dynamic_slice_in_dim(first, lane * near, near, 1)
    side_ints = jnp.concatenate([tn(own, own), tn(left, second)], 0)
    x_flips = [(0, 0), (1, 0)]
    x_index = aux & 1
    part = scatter_sum(side_ints, x_flips, x_index)
    start = x_index * part.shape[0]
    part, more = z_scatter(part)
    start = start + more
    row = start + jnp.arange(part.shape[0])
    in_own = row < virt
    a_index = jnp.where(in_own, row, row - virt + lane * near)
    occ_i = jnp.where(in_own, pick(occ_side, lane), occ_side[0])
    occ_j = jnp.where(in_own, pick(occ_side, lane), occ_side[1])
    weight = jnp.where(
        in_own, mask[pair, pair], mask[2 * side, 2 * side + 1])
    row_term = jnp.take(vir_energy, a_index) - occ_i - occ_j
    part = weight[:, None] * part / (row_term[:, None] + vir_energy[None, :])
    side_amps = gather(z_gather(part), x_flips, x_index)
    own_amps = side_amps[:virt]
    mixed = side_amps[virt:]
    mixed_twin = across(mixed, 0, 1)
    mixed_amps = jnp.concatenate(
        [jnp.where(lane == 0, mixed, mixed_twin), jnp.where(lane == 0, mixed_twin, mixed)], 0)

    here = pick(pieces, side)
    twin_here = pick(twin.reshape(2, half, virt), side)
    facing_twin = across(facing_near, 0, 1)
    low = jnp.where(side == 0, here, facing_near)
    high = jnp.where(side == 0, facing_near, here)
    high_twin = jnp.where(side == 0, facing_twin, twin_here)
    high_first = jnp.where(lane == 0, high, high_twin)
    high_second = jnp.where(lane == 0, high_twin, high)
    cross_ints = jnp.concatenate([tn(low, high_first), tn(low, high_second)], 0)
    q_flips = [(0, 0), (1, 0), (0, 2), (1, 2)]
    q_index = (aux & 1) + 2 * side
    part = scatter_sum(cross_ints, q_flips, q_index)
    start = q_index * part.shape[0]
    part, more = z_scatter(part)
    start = start + more
    row = start + jnp.arange(part.shape[0])
    block = row // virt
    a_index = row % virt
    weight = jnp.where(block == 0, mask[lane, 2], mask[lane, 3])
    row_term = jnp.take(vir_energy, a_index) - pick(occ_low, lane) - jnp.where(
        block == 0, occ_high[0], occ_high[1])
    part = weight[:, None] * part / (row_term[:, None] + vir_energy[None, :])
    cross_amps = gather(z_gather(part), q_flips, q_index)

    cross_blocks = cross_amps.reshape(2, virt, virt)
    swapped = across(pick(cross_blocks, lane ^ 1), 0, 1)
    kept = pick(cross_blocks, lane)
    facing_far_twin = across(facing_far, 0, 1)
    zero_near = jnp.where(side == 0, facing_near, facing_far)
    zero_far = jnp.where(side == 0, facing_far, facing_near)
    facing = jnp.concatenate([zero_near, zero_far], 0)
    twin_near = jnp.where(side == 0, facing_twin, facing_far_twin)
    twin_far = jnp.where(side == 0, facing_far_twin, facing_twin)
    facing_t = jnp.concatenate([twin_near, twin_far], 0)
    f_first = jnp.where(lane == 0, facing, facing_t)
    f_second = jnp.where(lane == 0, facing_t, facing)
    low_amps = jnp.where(lane == 0, kept, swapped)
    high_amps = jnp.where(lane == 0, swapped, kept)
    m0 = jnp.where(side == 0, cross_blocks[0], low_amps.T)
    m1 = jnp.where(side == 0, cross_blocks[1], high_amps.T)
    mixed_use = jnp.where(lane == 0, mixed_amps, mixed_amps.T)
    gamma = nt(own, own_amps) + nt(twin, mixed_use) + nt(f_first, m0) + nt(f_second, m1)
    return gamma.reshape(rows, occ_count, virt)


LANES = 128
IN_VMEM = pl.BlockSpec(memory_space=pltpu.VMEM)
IN_SMEM = pl.BlockSpec(memory_space=pltpu.SMEM)
SLOTS = (1, 2, 4)
WHOLE_SLOTS = 2
STEP = 512
SPARE_BYTES = 2 << 20


def dot_tn(left, right):
    return lax.dot_general(
        left, right, (((0,), (0,)), ((), ())), preferred_element_type=jnp.float32)


def dot_nn(left, right):
    return jnp.dot(left, right, preferred_element_type=jnp.float32)


def halves(value):
    top = value.astype(jnp.bfloat16)
    return top, (value - top.astype(jnp.float32)).astype(jnp.bfloat16)


def spots():
    aux, pair = lax.axis_index("aux"), lax.axis_index("pair")
    return aux & 1, aux >> 1, pair >> 1, pair & 1, pair


def call(kernel, outs, args, in_smem=(), scratch=(), flops=0):
    outs = [jax.ShapeDtypeStruct(o[:2], o[2] if len(o) > 2 else jnp.float32) for o in outs]
    scratch = [jax.ShapeDtypeStruct(*s) for s in scratch]
    moved = sum(a.size * a.dtype.itemsize for a in (*args, *outs))
    held = moved + sum(s.size * s.dtype.itemsize for s in scratch)
    return pl.pallas_call(
        kernel,
        out_shape=outs,
        in_specs=[IN_SMEM if i in in_smem else IN_VMEM for i in range(len(args))],
        out_specs=[IN_VMEM for _ in outs],
        scratch_shapes=[pltpu.VMEM(s.shape, s.dtype) for s in scratch],
        cost_estimate=pl.CostEstimate(flops=flops, bytes_accessed=moved, transcendentals=0),
        compiler_params=pltpu.CompilerParams(vmem_limit_bytes=held + SPARE_BYTES),
    )(*args)


def unpack(ref, rows, chunks, top_ref, low_ref):
    step = min(256, rows)

    @pl.loop(0, rows // step)
    def _(block):
        for c in range(chunks):
            top, low = halves(ref[pl.ds(block * step * chunks + c, step, stride=chunks), :])
            where = pl.ds(pl.multiple_of(block * step, step), step)
            top_ref[where, c * LANES:(c + 1) * LANES] = top
            low_ref[where, c * LANES:(c + 1) * LANES] = low


def half_rows(left, right, lane, chunks, spare):
    virt = chunks * LANES
    width = -(-chunks // 2) * LANES
    begin = lane * (chunks // 2) * LANES
    where = pl.ds(pl.multiple_of(begin, LANES), width)
    lt, ll = left[0][:, where], left[1][:, where]
    rt, rl = right[0][...], right[1][...]
    spare[...] = (dot_tn(rt, lt) + (dot_tn(rt, ll) + dot_tn(rl, lt))).T
    skip = lane * (virt // 2) - begin
    return spare[pl.ds(pl.multiple_of(skip, 8), virt // 2), :]


def own_kernel(rows, chunks, own, keep, send, top, low, acc, cross):
    x, _, _, _, _ = spots()
    unpack(own, rows, chunks, top, low)
    cross[...] = dot_tn(top[...], low[...])
    acc[...] = dot_tn(top[...], top[...]) + (cross[...] + cross[...].T)
    size = keep.shape[0]
    keep[...] = acc[pl.ds(pl.multiple_of(x * size, 8), size), :]
    send[...] = acc[pl.ds(pl.multiple_of((1 - x) * size, 8), size), :]


def twin_kernel(rows, chunks, own_top, own_low, twin, keep, send, top, low, acc, spare):
    x, _, _, lane, _ = spots()
    unpack(twin, rows, chunks, top, low)
    own, other = (own_top, own_low), (top, low)
    for here, left, right in ((0, own, other), (1, other, own)):

        @pl.when(lane == here)
        def _(here=here, left=left, right=right):
            acc[...] = half_rows(left, right, here, chunks, spare)

    size = keep.shape[0]
    keep[...] = acc[pl.ds(pl.multiple_of(x * size, 8), size), :]
    send[...] = acc[pl.ds(pl.multiple_of((1 - x) * size, 8), size), :]


def side_pair(mask, slot, slots):
    if slots == 4:
        return slot // 2, 2 + slot % 2, mask[slot // 2, 2 + slot % 2]
    count, found, weight = jnp.int32(0), jnp.int32(0), jnp.int32(0)
    for k in range(4):
        live = mask[k // 2, 2 + k % 2]
        hit = (live > 0) & (count == slot)
        found = jnp.where(hit, k, found)
        weight = jnp.where(hit, live, weight)
        count = count + (live > 0).astype(jnp.int32)
    return found // 2, 2 + found % 2, weight


def cross_kernel(half, chunks, mask, own_top, own_low, twin_top, twin_low, face, face_twin,
                 *rest):
    outs, (face_tops, face_lows), (top, low, acc, spare) = rest[:-6], rest[-6:-4], rest[-4:]
    x, _, side, lane, pair = spots()
    virt = chunks * LANES
    rows = pl.ds(pl.multiple_of(side * half, half), half)
    top[pair], low[pair] = own_top[rows, :], own_low[rows, :]
    top[pair ^ 1], low[pair ^ 1] = twin_top[rows, :], twin_low[rows, :]
    for ref, flip in ((face, 2), (face_twin, 3)):
        which = pair ^ flip
        unpack(ref, half, chunks, top.at[which], low.at[which])
        at = slice((flip - 2) * half, (flip - 1) * half)
        face_tops[at, :], face_lows[at, :] = top[which], low[which]
    live = jnp.int32(0)
    for k in range(4):
        live = live + (mask[k // 2, 2 + k % 2] > 0).astype(jnp.int32)
    square = x + 2 * side
    for number, slots in enumerate(SLOTS):
        fewer = SLOTS[number - 1] if number else 0

        @pl.when((live > fewer) & (live <= slots))
        def _(number=number, slots=slots):
            for slot in range(slots):
                first, second, _ = side_pair(mask, slot, slots)
                acc[slot * virt // 2:(slot + 1) * virt // 2, :] = half_rows(
                    (top.at[first], low.at[first]), (top.at[second], low.at[second]),
                    lane, chunks, spare)
            mine = outs[4 * number:4 * number + 4]
            size = mine[0].shape[0]
            for step in range(4):
                mine[step][...] = acc[
                    pl.ds(pl.multiple_of((square ^ step) * size, 8), size), :]


def add_kernel(members, sets, *refs):
    _, z, _, _, _ = spots()
    ins, outs = refs[:members * sets], refs[members * sets:]
    count = len(outs)
    at = 0
    for which in range(sets):
        mine = ins[which * members:(which + 1) * members]
        size = mine[0].shape[0] // count
        for step in range(count):
            where = pl.ds(pl.multiple_of((z ^ step) * size, 8), size)
            total = mine[0][where, :]
            for other in mine[1:]:
                total = total + other[where, :]
            outs[step][at:at + size, :] = total
        at += size


def sum_kernel(*refs):
    total = refs[0][...]
    for other in refs[1:-1]:
        total = total + other[...]
    refs[-1][...] = total


def join_kernel(sizes, *refs):
    _, z, _, _, _ = spots()
    out, ins = refs[-1], refs[:-1]
    inner = outer = 0
    for size in sizes:
        for step, piece in enumerate(ins):
            at = pl.multiple_of(outer + (z ^ step) * size, 8)
            out[pl.ds(at, size), :] = piece[inner:inner + size, :]
        inner += size
        outer += size * len(ins)


def scale_kernel(chunks, slots, members, cut, mask, occ, vir_row, vir_col, *refs):
    x, z, side, lane, pair = spots()
    ins, out = refs[:members], refs[members]
    virt = chunks * LANES
    size = out.shape[0]
    own_size = size * 2 // 3
    for group in range(size // 8):
        row = group * 8
        if slots == 0:
            mixed = row >= own_size
            if mixed:
                row = (x * members + z) * (size - own_size) + row - own_size
                first, second = 2 * side, 2 * side + 1
                origin = lane * (virt // 2) + row
            else:
                origin = (x * members + z) * own_size + row
                first = second = pair
            weight = mask[first, second]
        else:
            row = ((x + 2 * side) * (members if cut else 1) + (z if cut else 0)) * size + row
            first, second, weight = side_pair(mask, 0, slots)
            for slot in range(1, slots):
                f, s, w = side_pair(mask, slot, slots)
                here = row >= slot * virt // 2
                first = jnp.where(here, f, first)
                second = jnp.where(here, s, second)
                weight = jnp.where(here, w, weight)
            origin = lane * (virt // 2) + row % (virt // 2)
        here = slice(group * 8, group * 8 + 8)
        total = ins[0][here, :]
        for other in ins[1:]:
            total = total + other[here, :]
        energy = vir_col[pl.ds(pl.multiple_of(origin, 8), 8), :] + vir_row[...]
        energy = energy - occ[first] - occ[second]
        out[here, :] = weight.astype(jnp.float32) * total / energy


def place_block(halves_ref, first, chunks, whole):
    part = chunks * LANES // 2
    for lane in range(2):
        whole[lane * part:(lane + 1) * part, :] = halves_ref[lane, pl.ds(first, part), :]


def wide(top, low):
    return jnp.concatenate([top, low, top], 1)


def stack(value, stacked):
    virt = value.shape[0]
    top, low = halves(value)
    stacked[0:virt, :] = top
    stacked[virt:2 * virt, :] = top
    stacked[2 * virt:3 * virt, :] = low


def near_gamma_kernel(rows, chunks, own_top, own_low, twin_top, twin_low,
                      keep, other, keep_t, other_t, out, parts, whole, stacked):
    x, _, _, lane, _ = spots()
    virt = chunks * LANES
    size = keep.shape[0]
    own_size = size * 2 // 3
    mixed = size - own_size
    for ref, slot, piece in ((keep, lane, x), (other, lane, 1 - x),
                             (keep_t, 1 - lane, x), (other_t, 1 - lane, 1 - x)):
        parts[slot, pl.ds(pl.multiple_of(piece * own_size, 8), own_size), :] = ref[:own_size, :]
        parts[slot, pl.ds(pl.multiple_of(virt + piece * mixed, 8), mixed), :] = ref[own_size:, :]
    stack(parts[lane, 0:virt, :], stacked.at[0])
    place_block(parts, virt, chunks, whole)

    @pl.when(lane == 0)
    def _():
        stack(whole[...].T, stacked.at[1])

    @pl.when(lane == 1)
    def _():
        stack(whole[...], stacked.at[1])

    step = min(STEP, rows)

    @pl.loop(0, rows // step)
    def _(block):
        at = pl.ds(pl.multiple_of(block * step, step), step)
        out[at, :] = dot_nn(wide(own_top[at, :], own_low[at, :]), stacked[0]) + dot_nn(
            wide(twin_top[at, :], twin_low[at, :]), stacked[1])


def far_gamma_kernel(rows, chunks, slots, mask, base, face_tops, face_lows, far, far_t, *rest):
    pieces, pieces_t = rest[0:4], rest[4:8]
    out, parts, whole, stacked, total = rest[8:]
    x, _, side, lane, pair = spots()
    virt = chunks * LANES
    half = rows // 2
    size = pieces[0].shape[0]
    square = x + 2 * side
    for step in range(4):
        where = pl.ds(pl.multiple_of((square ^ step) * size, 8), size)
        parts[lane, where, :] = pieces[step][...]
        parts[1 - lane, where, :] = pieces_t[step][...]
    step = min(STEP, half)
    total[...] = base[...]
    for flip in (0, 1):
        partner = pair ^ (2 + flip)
        first = jnp.minimum(pair, partner)
        second = jnp.maximum(pair, partner)
        live, at = jnp.int32(0), jnp.int32(0)
        for slot in range(slots):
            f, s, weight = side_pair(mask, slot, slots)
            hit = (f == first) & (s == second) & (weight > 0)
            live = jnp.where(hit, 1, live)
            at = jnp.where(hit, slot, at)

        @pl.when(live > 0)
        def _(flip=flip, at=at):
            place_block(parts, pl.multiple_of(at * (virt // 2), 8), chunks, whole)

            @pl.when(side == 0)
            def _():
                stack(whole[...].T, stacked)

            @pl.when(side == 1)
            def _():
                stack(whole[...], stacked)

            @pl.loop(0, half // step)
            def _(block):
                rows_in = pl.ds(pl.multiple_of(flip * half + block * step, step), step)
                rows_out = pl.ds(pl.multiple_of(side * half + block * step, step), step)
                total[rows_out, :] += dot_nn(
                    wide(face_tops[rows_in, :], face_lows[rows_in, :]), stacked[...])
                source = far_t if flip else far
                parts_in = [
                    halves(source[pl.ds(block * step * chunks + c, step, stride=chunks), :])
                    for c in range(chunks)]
                tops, lows = [p[0] for p in parts_in], [p[1] for p in parts_in]
                rows_out = pl.ds(pl.multiple_of((1 - side) * half + block * step, step), step)
                total[rows_out, :] += dot_nn(
                    jnp.concatenate(tops + lows + tops, 1), stacked[...])

    flat_kernel(rows, chunks, total, out)


def flat_kernel(rows, chunks, base, out):
    step = min(256, rows)

    @pl.loop(0, rows // step)
    def _(block):
        at = block * step
        for c in range(chunks):
            out[pl.ds(at * chunks + c, step, stride=chunks), :] = base[
                pl.ds(pl.multiple_of(at, step), step), c * LANES:(c + 1) * LANES]


def pick_branch(pair_mask):
    live = jnp.sum((pair_mask[:2, 2:] > 0).astype(jnp.int32))
    branch = jnp.int32(0)
    for slots in (0, *SLOTS[:-1]):
        branch = branch + (live > slots).astype(jnp.int32)
    return branch


def opening(three_center, occ_energy, pair_mask):
    rows, _, virt = three_center.shape
    chunks = virt // LANES
    half = rows // 2
    z_count = lax.axis_size("aux") // 2
    pair = lax.axis_index("pair")
    side, lane = pair // 2, pair % 2
    own = three_center.reshape(rows * chunks, LANES)
    bf16, f32 = jnp.bfloat16, jnp.float32
    block_flops = 6 * rows * virt * virt
    flat_pieces = own.reshape(2, half * chunks, LANES)
    near = across(pick(flat_pieces, 1 - side), 0, 2)
    twin = across(own, 0, 1)
    split = [(rows, virt, bf16)] * 2
    mixed_rows = virt // 2
    keep_a, send_a, own_top, own_low = call(
        functools.partial(own_kernel, rows, chunks), [(virt // 2, virt)] * 2 + split, [own],
        scratch=[((virt, virt), f32)] * 2, flops=block_flops)
    got_a = across(send_a, 1, 0)
    twin, send_a = lax.optimization_barrier((twin, send_a))
    keep_b, send_b, twin_top, twin_low = call(
        functools.partial(twin_kernel, rows, chunks), [(mixed_rows // 2, virt)] * 2 + split,
        [own_top, own_low, twin],
        scratch=[((mixed_rows, virt), f32), ((-(-chunks // 2) * LANES, virt), f32)],
        flops=block_flops)
    got_b = across(send_b, 1, 0)
    occ_energy, send_b = lax.optimization_barrier((occ_energy, send_b))
    got_a, later_mask = lax.optimization_barrier((got_a, pair_mask))
    branch = pick_branch(later_mask)
    occ_side = jnp.concatenate([occ_energy, across(occ_energy, 0, 1)])
    occ_side = jnp.where(lane == 0, occ_side, occ_side[::-1])
    occ_other = across(occ_side, 0, 2)
    occ = jnp.where(side == 0, jnp.concatenate([occ_side, occ_other]),
                    jnp.concatenate([occ_other, occ_side]))
    later_own, _ = lax.optimization_barrier((own, send_b))
    far_send = pick(later_own.reshape(2, half * chunks, LANES), side)
    keep_a, branch, far_send = lax.optimization_barrier((keep_a, branch, far_send))
    piece_rows = (virt + mixed_rows) // 2 // z_count
    pieces = call(functools.partial(add_kernel, 2, 2), [(piece_rows, virt)] * z_count,
                   [keep_a, got_a, keep_b, got_b])
    side_got = [across(pieces[s], s << 1, 0) for s in range(1, z_count)]
    near_t = across(near, 0, 1)
    most = SLOTS[-1] * mixed_rows
    cross = call(
        functools.partial(cross_kernel, half, chunks),
        [(n * mixed_rows // 4, virt) for n in SLOTS for _ in range(4)] + split,
        [pair_mask, own_top, own_low, twin_top, twin_low, near, near_t], in_smem=(0,),
        scratch=[((4, half, virt), bf16)] * 2 + [
            ((most, virt), f32), ((-(-chunks // 2) * LANES, virt), f32)],
        flops=block_flops)
    cross, faces = cross[:-2], cross[-2:]
    return lax.optimization_barrier((
        (own_top, own_low, twin_top, twin_low), faces, far_send, occ,
        [pieces[0], *side_got], cross)), branch


def closing(slots, shape, opened, vir_row, vir_col, pair_mask):
    splits, faces, far_send, occ, side_parts, cross = opened
    rows, _, virt = shape
    chunks = virt // LANES
    z_count = lax.axis_size("aux") // 2
    bf16, f32 = jnp.bfloat16, jnp.float32
    block_flops = 6 * rows * virt * virt
    energies = [pair_mask, occ, vir_row, vir_col]
    piece_rows = side_parts[0].shape[0]
    own_size = piece_rows * 2 // 3
    total_rows = slots * virt // 2
    square_rows = total_rows // 4
    slab_rows = square_rows // z_count
    flips = [(0, 0), (1, 0), (0, 2), (1, 2)]

    def z_spread(slab, relay):
        got = {0: slab}
        for s in range(1, z_count):
            direct = s & (s - 1) == 0 or not relay
            got[s] = across(got[0 if direct else s & (s - 1)],
                           (s if direct else s & -s) << 1, 0)
        return [got[s] for s in range(1, z_count)]

    if slots:
        at = 4 * SLOTS.index(slots)
        cross = cross[at:at + 4]
        cross_got = [across(cross[s], *flips[s]) for s in range(1, 4)]
    slab, = call(
        functools.partial(scale_kernel, chunks, 0, z_count, True),
        [(piece_rows, virt)], [*energies, *side_parts], in_smem=(0, 1))
    side_slabs = [slab] + z_spread(slab, False)
    joined, = call(
        functools.partial(join_kernel, (own_size, piece_rows - own_size)),
        [(piece_rows * z_count, virt)], side_slabs)
    other = across(joined, 1, 0)
    joined_t = across(joined, 0, 1)
    other_t = across(other, 0, 1)
    gamma, = call(
        functools.partial(near_gamma_kernel, rows, chunks), [(rows, virt)],
        [*splits, joined, other, joined_t, other_t],
        scratch=[((2, virt + virt // 2, virt), f32), ((virt, virt), f32),
                 ((2, 3 * virt, virt), bf16)], flops=2 * block_flops)
    if not slots:
        gamma, = call(functools.partial(flat_kernel, rows, chunks), [(rows * chunks, LANES)],
                      [gamma])
        return gamma
    if slots <= WHOLE_SLOTS:
        summed, = call(sum_kernel, [(square_rows, virt)], [cross[0], *cross_got])
        z_got = z_spread(summed, True)
        joined_c, = call(
            functools.partial(scale_kernel, chunks, slots, z_count, False),
            [(square_rows, virt)], [*energies, summed, *z_got], in_smem=(0, 1))
    else:
        pieces_c = call(
            functools.partial(add_kernel, 4, 1), [(slab_rows, virt)] * z_count,
            [cross[0], *cross_got])
        summed = pieces_c[0]
        z_got = [across(pieces_c[s], s << 1, 0) for s in range(1, z_count)]
        cross_slab, = call(
            functools.partial(scale_kernel, chunks, slots, z_count, True),
            [(slab_rows, virt)], [*energies, pieces_c[0], *z_got], in_smem=(0, 1))
        joined_c, = call(
            functools.partial(join_kernel, (slab_rows,)), [(square_rows, virt)],
            [cross_slab] + z_spread(cross_slab, False))
    far_send, summed = lax.optimization_barrier((far_send, summed))
    far = across(far_send, 0, 2)
    far_t = across(far, 0, 1)
    whole = [across(joined_c, *flips[s]) for s in range(1, 4)]
    joined_ct = across(joined_c, 0, 1)
    whole_t = [across(piece, 0, 1) for piece in whole]
    gamma, = call(
        functools.partial(far_gamma_kernel, rows, chunks, slots),
        [(rows * chunks, LANES)],
        [pair_mask, gamma, *faces, far, far_t, joined_c, *whole, joined_ct, *whole_t],
        in_smem=(0,),
        scratch=[((2, total_rows, virt), f32), ((virt, virt), f32),
                 ((3 * virt, virt), bf16), ((rows, virt), f32)],
        flops=2 * block_flops)
    return gamma


def on_device(three_center, occ_energy, vir_energy, pair_mask):
    rows, occ_count, virt = three_center.shape
    aux_count, pair_count = lax.axis_size("aux"), lax.axis_size("pair")
    z_count = aux_count // 2
    fits = (
        occ_count == 1 and pair_count == 4 and z_count in (2, 4) and aux_count == 2 * z_count
        and virt % LANES == 0 and rows % 16 == 0
        and virt % (8 * z_count * 8 // 2) == 0 and (virt + virt // 2) % (16 * z_count) == 0)
    args = (three_center, occ_energy, vir_energy, pair_mask)
    if not fits:
        return general_path(*args)
    opened, branch = opening(three_center, occ_energy, pair_mask)
    gamma = lax.switch(
        branch, [functools.partial(closing, n, three_center.shape)
                 for n in (0, *SLOTS)],
        opened, vir_energy.reshape(1, virt), vir_energy.reshape(virt, 1), pair_mask)
    return gamma.reshape(three_center.shape)


def solution(mesh):
    in_specs = (P("aux", "pair", None), P("pair"), P(), P())
    out_specs = P("aux", "pair", None)
    return jax.shard_map(
        on_device, mesh=mesh, in_specs=in_specs, out_specs=out_specs, check_vma=False
    )
```

```python
import functools

import jax
import jax.numpy as jnp
from jax import lax
from jax.experimental import pallas as pl
from jax.experimental.pallas import tpu as pltpu
from jax.sharding import PartitionSpec as P

AXES = ("aux", "pair")
precision = lax.Precision.HIGH


def across(value, aux_flip, pair_flip):
    aux_count, pair_count = lax.axis_size("aux"), lax.axis_size("pair")
    moves = [
        (a * pair_count + p, (a ^ aux_flip) * pair_count + (p ^ pair_flip))
        for a in range(aux_count)
        for p in range(pair_count)
    ]
    return lax.ppermute(value, AXES, moves)


def pick(pieces, index):
    return lax.dynamic_index_in_dim(pieces, index, 0, keepdims=False)


def tn(left, right):
    return lax.dot_general(
        left, right, (((0,), (0,)), ((), ())), precision=precision,
        preferred_element_type=jnp.float32)


def nt(left, right):
    return lax.dot_general(
        left, right, (((1,), (1,)), ((), ())), precision=precision,
        preferred_element_type=jnp.float32)


def scatter_sum(value, flips, index):
    members = len(flips)
    pieces = value.reshape((members, value.shape[0] // members) + value.shape[1:])
    total = pick(pieces, index)
    for step in range(1, members):
        total = total + across(pick(pieces, index ^ step), *flips[step])
    return total


def gather(piece, flips, index):
    members = len(flips)
    whole = jnp.zeros((members,) + piece.shape, piece.dtype)
    whole = lax.dynamic_update_index_in_dim(whole, piece, index, 0)
    for step in range(1, members):
        whole = lax.dynamic_update_index_in_dim(
            whole, across(piece, *flips[step]), index ^ step, 0)
    return whole.reshape((members * piece.shape[0],) + piece.shape[1:])


def aux_groups(aux_count):
    bits = aux_count.bit_length() - 1
    low, groups = 1, []
    while low < bits:
        width = min(2, bits - low)
        groups.append((low, width))
        low += width
    return groups


def general_path(three_center, occ_energy, vir_energy, pair_mask):
    rows, occ_count, virt = three_center.shape
    aux_count = lax.axis_size("aux")
    aux, pair = lax.axis_index("aux"), lax.axis_index("pair")
    side, lane = pair // 2, pair % 2
    half = rows // 2
    own = three_center.reshape(rows, virt)
    pieces = own.reshape(2, half, virt)
    occ_side = jnp.stack([occ_energy[0], across(occ_energy, 0, 1)[0]])
    occ_side = jnp.where(lane == 0, occ_side, occ_side[::-1])
    occ_other = across(occ_side, 0, 2)
    occ_low = jnp.where(side == 0, occ_side, occ_other)
    occ_high = jnp.where(side == 0, occ_other, occ_side)
    mask = pair_mask.astype(jnp.float32)

    facing_near = across(pick(pieces, side ^ 1), 0, 2)
    twin = across(own, 0, 1)
    facing_far = across(pick(pieces, side), 0, 2)

    z_groups = aux_groups(aux_count)

    def z_scatter(value):
        start = jnp.int32(0)
        for low, width in z_groups:
            members = 1 << width
            index = (aux >> low) & (members - 1)
            value = scatter_sum(value, [(s << low, 0) for s in range(members)], index)
            start = start + index * value.shape[0]
        return value, start

    def z_gather(value):
        for low, width in reversed(z_groups):
            members = 1 << width
            index = (aux >> low) & (members - 1)
            value = gather(value, [(s << low, 0) for s in range(members)], index)
        return value

    first = jnp.where(lane == 0, own, twin)
    second = jnp.where(lane == 0, twin, own)
    near = virt // 2
    left = lax.dynamic_slice_in_dim(first, lane * near, near, 1)
    side_ints = jnp.concatenate([tn(own, own), tn(left, second)], 0)
    x_flips = [(0, 0), (1, 0)]
    x_index = aux & 1
    part = scatter_sum(side_ints, x_flips, x_index)
    start = x_index * part.shape[0]
    part, more = z_scatter(part)
    start = start + more
    row = start + jnp.arange(part.shape[0])
    in_own = row < virt
    a_index = jnp.where(in_own, row, row - virt + lane * near)
    occ_i = jnp.where(in_own, pick(occ_side, lane), occ_side[0])
    occ_j = jnp.where(in_own, pick(occ_side, lane), occ_side[1])
    weight = jnp.where(
        in_own, mask[pair, pair], mask[2 * side, 2 * side + 1])
    row_term = jnp.take(vir_energy, a_index) - occ_i - occ_j
    part = weight[:, None] * part / (row_term[:, None] + vir_energy[None, :])
    side_amps = gather(z_gather(part), x_flips, x_index)
    own_amps = side_amps[:virt]
    mixed = side_amps[virt:]
    mixed_twin = across(mixed, 0, 1)
    mixed_amps = jnp.concatenate(
        [jnp.where(lane == 0, mixed, mixed_twin), jnp.where(lane == 0, mixed_twin, mixed)], 0)

    here = pick(pieces, side)
    twin_here = pick(twin.reshape(2, half, virt), side)
    facing_twin = across(facing_near, 0, 1)
    low = jnp.where(side == 0, here, facing_near)
    high = jnp.where(side == 0, facing_near, here)
    high_twin = jnp.where(side == 0, facing_twin, twin_here)
    high_first = jnp.where(lane == 0, high, high_twin)
    high_second = jnp.where(lane == 0, high_twin, high)
    cross_ints = jnp.concatenate([tn(low, high_first), tn(low, high_second)], 0)
    q_flips = [(0, 0), (1, 0), (0, 2), (1, 2)]
    q_index = (aux & 1) + 2 * side
    part = scatter_sum(cross_ints, q_flips, q_index)
    start = q_index * part.shape[0]
    part, more = z_scatter(part)
    start = start + more
    row = start + jnp.arange(part.shape[0])
    block = row // virt
    a_index = row % virt
    weight = jnp.where(block == 0, mask[lane, 2], mask[lane, 3])
    row_term = jnp.take(vir_energy, a_index) - pick(occ_low, lane) - jnp.where(
        block == 0, occ_high[0], occ_high[1])
    part = weight[:, None] * part / (row_term[:, None] + vir_energy[None, :])
    cross_amps = gather(z_gather(part), q_flips, q_index)

    cross_blocks = cross_amps.reshape(2, virt, virt)
    swapped = across(pick(cross_blocks, lane ^ 1), 0, 1)
    kept = pick(cross_blocks, lane)
    facing_far_twin = across(facing_far, 0, 1)
    zero_near = jnp.where(side == 0, facing_near, facing_far)
    zero_far = jnp.where(side == 0, facing_far, facing_near)
    facing = jnp.concatenate([zero_near, zero_far], 0)
    twin_near = jnp.where(side == 0, facing_twin, facing_far_twin)
    twin_far = jnp.where(side == 0, facing_far_twin, facing_twin)
    facing_t = jnp.concatenate([twin_near, twin_far], 0)
    f_first = jnp.where(lane == 0, facing, facing_t)
    f_second = jnp.where(lane == 0, facing_t, facing)
    low_amps = jnp.where(lane == 0, kept, swapped)
    high_amps = jnp.where(lane == 0, swapped, kept)
    m0 = jnp.where(side == 0, cross_blocks[0], low_amps.T)
    m1 = jnp.where(side == 0, cross_blocks[1], high_amps.T)
    mixed_use = jnp.where(lane == 0, mixed_amps, mixed_amps.T)
    gamma = nt(own, own_amps) + nt(twin, mixed_use) + nt(f_first, m0) + nt(f_second, m1)
    return gamma.reshape(rows, occ_count, virt)


LANES = 128
IN_VMEM = pl.BlockSpec(memory_space=pltpu.VMEM)
IN_SMEM = pl.BlockSpec(memory_space=pltpu.SMEM)
SLOTS = (1, 2, 4)
WHOLE_SLOTS = 4
STEP = 512
SPARE_BYTES = 2 << 20


def dot_tn(left, right):
    return lax.dot_general(
        left, right, (((0,), (0,)), ((), ())), preferred_element_type=jnp.float32)


def dot_nn(left, right):
    return jnp.dot(left, right, preferred_element_type=jnp.float32)


def halves(value):
    top = value.astype(jnp.bfloat16)
    return top, (value - top.astype(jnp.float32)).astype(jnp.bfloat16)


def spots():
    aux, pair = lax.axis_index("aux"), lax.axis_index("pair")
    return aux & 1, aux >> 1, pair >> 1, pair & 1, pair


def call(kernel, outs, args, in_smem=(), scratch=(), flops=0):
    outs = [jax.ShapeDtypeStruct(o[:2], o[2] if len(o) > 2 else jnp.float32) for o in outs]
    scratch = [jax.ShapeDtypeStruct(*s) for s in scratch]
    moved = sum(a.size * a.dtype.itemsize for a in (*args, *outs))
    held = moved + sum(s.size * s.dtype.itemsize for s in scratch)
    return pl.pallas_call(
        kernel,
        out_shape=outs,
        in_specs=[IN_SMEM if i in in_smem else IN_VMEM for i in range(len(args))],
        out_specs=[IN_VMEM for _ in outs],
        scratch_shapes=[pltpu.VMEM(s.shape, s.dtype) for s in scratch],
        cost_estimate=pl.CostEstimate(flops=flops, bytes_accessed=moved, transcendentals=0),
        compiler_params=pltpu.CompilerParams(vmem_limit_bytes=held + SPARE_BYTES),
    )(*args)


def unpack(ref, rows, chunks, top_ref, low_ref):
    step = min(256, rows)

    @pl.loop(0, rows // step)
    def _(block):
        for c in range(chunks):
            top, low = halves(ref[pl.ds(block * step * chunks + c, step, stride=chunks), :])
            where = pl.ds(pl.multiple_of(block * step, step), step)
            top_ref[where, c * LANES:(c + 1) * LANES] = top
            low_ref[where, c * LANES:(c + 1) * LANES] = low


def half_rows(left, right, lane, chunks, spare):
    virt = chunks * LANES
    width = -(-chunks // 2) * LANES
    begin = lane * (chunks // 2) * LANES
    where = pl.ds(pl.multiple_of(begin, LANES), width)
    lt, ll = left[0][:, where], left[1][:, where]
    rt, rl = right[0][...], right[1][...]
    spare[...] = (dot_tn(rt, lt) + (dot_tn(rt, ll) + dot_tn(rl, lt))).T
    skip = lane * (virt // 2) - begin
    return spare[pl.ds(pl.multiple_of(skip, 8), virt // 2), :]


def packed_rows(chunks):
    return (chunks + 1) // 2 * LANES


def own_share(size, chunks):
    packed = packed_rows(chunks)
    return size * packed // (packed + chunks * LANES // 2)


def triangle_parts(chunks):
    for r in range((chunks + 1) // 2):
        yield r, 0, r
        if r:
            yield r, (chunks - r) * LANES, chunks - r


def own_kernel(rows, chunks, own, keep, send, top, low, acc, cross, packed):
    x, _, _, _, _ = spots()
    unpack(own, rows, chunks, top, low)
    cross[...] = dot_tn(top[...], low[...])
    acc[...] = dot_tn(top[...], top[...]) + (cross[...] + cross[...].T)
    for r, column, block in triangle_parts(chunks):
        width = (chunks - block) * LANES
        packed[r * LANES:(r + 1) * LANES, column:column + width] = acc[
            block * LANES:(block + 1) * LANES, block * LANES:]
    size = keep.shape[0]
    keep[...] = packed[pl.ds(pl.multiple_of(x * size, 8), size), :]
    send[...] = packed[pl.ds(pl.multiple_of((1 - x) * size, 8), size), :]


def twin_kernel(rows, chunks, own_top, own_low, twin, keep, send, top, low, acc, spare):
    x, _, _, lane, _ = spots()
    unpack(twin, rows, chunks, top, low)
    own, other = (own_top, own_low), (top, low)
    for here, left, right in ((0, own, other), (1, other, own)):

        @pl.when(lane == here)
        def _(here=here, left=left, right=right):
            acc[...] = half_rows(left, right, here, chunks, spare)

    size = keep.shape[0]
    keep[...] = acc[pl.ds(pl.multiple_of(x * size, 8), size), :]
    send[...] = acc[pl.ds(pl.multiple_of((1 - x) * size, 8), size), :]


def side_pair(mask, slot, slots):
    if slots == 4:
        return slot // 2, 2 + slot % 2, mask[slot // 2, 2 + slot % 2]
    count, found, weight = jnp.int32(0), jnp.int32(0), jnp.int32(0)
    for k in range(4):
        live = mask[k // 2, 2 + k % 2]
        hit = (live > 0) & (count == slot)
        found = jnp.where(hit, k, found)
        weight = jnp.where(hit, live, weight)
        count = count + (live > 0).astype(jnp.int32)
    return found // 2, 2 + found % 2, weight


def cross_kernel(half, chunks, mask, own_top, own_low, twin_top, twin_low, face, face_twin,
                 *rest):
    outs, (face_tops, face_lows), (top, low, acc, spare) = rest[:-6], rest[-6:-4], rest[-4:]
    x, _, side, lane, pair = spots()
    virt = chunks * LANES
    rows = pl.ds(pl.multiple_of(side * half, half), half)
    top[pair], low[pair] = own_top[rows, :], own_low[rows, :]
    top[pair ^ 1], low[pair ^ 1] = twin_top[rows, :], twin_low[rows, :]
    for ref, flip in ((face, 2), (face_twin, 3)):
        which = pair ^ flip
        unpack(ref, half, chunks, top.at[which], low.at[which])
        at = slice((flip - 2) * half, (flip - 1) * half)
        face_tops[at, :], face_lows[at, :] = top[which], low[which]
    live = jnp.int32(0)
    for k in range(4):
        live = live + (mask[k // 2, 2 + k % 2] > 0).astype(jnp.int32)
    square = x + 2 * side
    for number, slots in enumerate(SLOTS):
        fewer = SLOTS[number - 1] if number else 0

        @pl.when((live > fewer) & (live <= slots))
        def _(number=number, slots=slots):
            for slot in range(slots):
                first, second, _ = side_pair(mask, slot, slots)
                acc[slot * virt // 2:(slot + 1) * virt // 2, :] = half_rows(
                    (top.at[first], low.at[first]), (top.at[second], low.at[second]),
                    lane, chunks, spare)
            mine = outs[4 * number:4 * number + 4]
            size = mine[0].shape[0]
            for step in range(4):
                mine[step][...] = acc[
                    pl.ds(pl.multiple_of((square ^ step) * size, 8), size), :]


def add_kernel(members, sets, *refs):
    _, z, _, _, _ = spots()
    ins, outs = refs[:members * sets], refs[members * sets:]
    count = len(outs)
    at = 0
    for which in range(sets):
        mine = ins[which * members:(which + 1) * members]
        size = mine[0].shape[0] // count
        for step in range(count):
            where = pl.ds(pl.multiple_of((z ^ step) * size, 8), size)
            total = mine[0][where, :]
            for other in mine[1:]:
                total = total + other[where, :]
            outs[step][at:at + size, :] = total
        at += size


def x_add_kernel(vir, *refs):
    vir_row, vir_col = refs[-2:]
    virt = vir.shape[1]
    vir_row[:, :virt] = vir[...]
    vir_row[:, virt:] = vir[...]
    vir_col[...] = jnp.broadcast_to(vir[...], (LANES, virt)).T
    add_kernel(2, 2, *refs[:-2])


def sum_kernel(*refs):
    total = refs[0][...]
    for other in refs[1:-1]:
        total = total + other[...]
    refs[-1][...] = total


def join_kernel(sizes, *refs):
    _, z, _, _, _ = spots()
    out, ins = refs[-1], refs[:-1]
    inner = outer = 0
    for size in sizes:
        for step, piece in enumerate(ins):
            at = pl.multiple_of(outer + (z ^ step) * size, 8)
            out[pl.ds(at, size), :] = piece[inner:inner + size, :]
        inner += size
        outer += size * len(ins)


def scale_kernel(chunks, slots, members, cut, mask, occ_side, occ_other, vir_row, vir_col,
                 *refs):
    x, z, side, lane, pair = spots()
    ins, out = refs[:members], refs[members]

    def occ(which):
        mine, lane_of = (which >> 1) == side, which & 1
        return jnp.where(mine, occ_side[lane_of], occ_other[lane_of])

    virt = chunks * LANES
    size = out.shape[0]
    own_size = own_share(size, chunks)
    lanes = lax.broadcasted_iota(jnp.int32, (8, virt), 1)
    for group in range(size // 8):
        row = group * 8
        packed = slots == 0 and row < own_size
        if packed:
            row = (x * members + z) * own_size + row
            tile, inner = row >> (LANES.bit_length() - 1), row & (LANES - 1)
            first = second = pair
            weight = mask[pair, pair]
        elif slots == 0:
            row = (x * members + z) * (size - own_size) + row - own_size
            first, second = 2 * side, 2 * side + 1
            weight = mask[first, second]
            origin = lane * (virt // 2) + row
        else:
            row = ((x + 2 * side) * (members if cut else 1) + (z if cut else 0)) * size + row
            first, second, weight = side_pair(mask, 0, slots)
            inner = row
            for slot in range(1, slots):
                f, s, w = side_pair(mask, slot, slots)
                here = row >= slot * (virt // 2)
                first = jnp.where(here, f, first)
                second = jnp.where(here, s, second)
                weight = jnp.where(here, w, weight)
                inner = jnp.where(here, row - slot * (virt // 2), inner)
            origin = lane * (virt // 2) + inner
        here = slice(group * 8, group * 8 + 8)
        total = ins[0][here, :]
        for other in ins[1:]:
            total = total + other[here, :]
        if packed:
            ahead = pl.multiple_of(tile * LANES, LANES)
            behind = jnp.minimum(virt - tile * LANES, virt - LANES)
            energy = jnp.where(
                lanes < virt - tile * LANES,
                vir_col[pl.ds(pl.multiple_of(ahead + inner, 8), 8), 0:1]
                + vir_row[:, pl.ds(ahead, virt)],
                vir_col[pl.ds(pl.multiple_of(behind + inner, 8), 8), 0:1] + vir_row[:, :virt])
        else:
            energy = vir_col[pl.ds(pl.multiple_of(origin, 8), 8), 0:1] + vir_row[:, :virt]
        energy = energy - occ(first) - occ(second)
        out[here, :] = weight.astype(jnp.float32) * total / energy


def place_block(halves_ref, first, chunks, whole):
    part = chunks * LANES // 2
    for lane in range(2):
        whole[lane * part:(lane + 1) * part, :] = halves_ref[lane, pl.ds(first, part), :]


def wide(top, low):
    return jnp.concatenate([top, low, top], 1)


def stack(value, stacked):
    virt = value.shape[0]
    top, low = halves(value)
    stacked[0:virt, :] = top
    stacked[virt:2 * virt, :] = top
    stacked[2 * virt:3 * virt, :] = low


def near_gamma_kernel(rows, chunks, own_top, own_low, twin_top, twin_low,
                      keep, other, keep_t, other_t, out, parts, whole, stacked):
    x, _, _, lane, _ = spots()
    size = keep.shape[0]
    own_size = own_share(size, chunks)
    mixed = size - own_size
    mixed_start = packed_rows(chunks)
    for ref, slot, piece in ((keep, lane, x), (other, lane, 1 - x),
                             (keep_t, 1 - lane, x), (other_t, 1 - lane, 1 - x)):
        parts[slot, pl.ds(pl.multiple_of(piece * own_size, 8), own_size), :] = ref[:own_size, :]
        parts[slot, pl.ds(pl.multiple_of(mixed_start + piece * mixed, 8), mixed), :] = ref[own_size:, :]
    for r, column, block in triangle_parts(chunks):
        for other_block in range(block, chunks):
            at = column + (other_block - block) * LANES
            tile = parts[lane, r * LANES:(r + 1) * LANES, at:at + LANES]
            mine, theirs = (slice(b * LANES, (b + 1) * LANES) for b in (block, other_block))
            whole[mine, theirs] = tile
            if other_block != block:
                whole[theirs, mine] = tile.T
    stack(whole[...], stacked.at[0])
    place_block(parts, mixed_start, chunks, whole)

    @pl.when(lane == 0)
    def _():
        stack(whole[...].T, stacked.at[1])

    @pl.when(lane == 1)
    def _():
        stack(whole[...], stacked.at[1])

    step = min(STEP, rows)

    @pl.loop(0, rows // step)
    def _(block):
        at = pl.ds(pl.multiple_of(block * step, step), step)
        out[at, :] = dot_nn(wide(own_top[at, :], own_low[at, :]), stacked[0]) + dot_nn(
            wide(twin_top[at, :], twin_low[at, :]), stacked[1])


def far_gamma_kernel(rows, chunks, slots, mask, base, face_tops, face_lows, far, far_t, *rest):
    pieces, pieces_t = rest[0:4], rest[4:8]
    out, parts, whole, stacked, total = rest[8:]
    x, _, side, lane, pair = spots()
    virt = chunks * LANES
    half = rows // 2
    size = pieces[0].shape[0]
    square = x + 2 * side
    for step in range(4):
        where = pl.ds(pl.multiple_of((square ^ step) * size, 8), size)
        parts[lane, where, :] = pieces[step][...]
        parts[1 - lane, where, :] = pieces_t[step][...]
    step = min(STEP, half)
    total[...] = base[...]
    for flip in (0, 1):
        partner = pair ^ (2 + flip)
        first = jnp.minimum(pair, partner)
        second = jnp.maximum(pair, partner)
        live, at = jnp.int32(0), jnp.int32(0)
        for slot in range(slots):
            f, s, weight = side_pair(mask, slot, slots)
            hit = (f == first) & (s == second) & (weight > 0)
            live = jnp.where(hit, 1, live)
            at = jnp.where(hit, slot, at)

        @pl.when(live > 0)
        def _(flip=flip, at=at):
            place_block(parts, pl.multiple_of(at * (virt // 2), 8), chunks, whole)

            @pl.when(side == 0)
            def _():
                stack(whole[...].T, stacked)

            @pl.when(side == 1)
            def _():
                stack(whole[...], stacked)

            @pl.loop(0, half // step)
            def _(block):
                rows_in = pl.ds(pl.multiple_of(flip * half + block * step, step), step)
                rows_out = pl.ds(pl.multiple_of(side * half + block * step, step), step)
                total[rows_out, :] += dot_nn(
                    wide(face_tops[rows_in, :], face_lows[rows_in, :]), stacked[...])
                source = far_t if flip else far
                parts_in = [
                    halves(source[pl.ds(block * step * chunks + c, step, stride=chunks), :])
                    for c in range(chunks)]
                tops, lows = [p[0] for p in parts_in], [p[1] for p in parts_in]
                rows_out = pl.ds(pl.multiple_of((1 - side) * half + block * step, step), step)
                total[rows_out, :] += dot_nn(
                    jnp.concatenate(tops + lows + tops, 1), stacked[...])

    flat_kernel(rows, chunks, total, out)


def flat_kernel(rows, chunks, base, out):
    step = min(256, rows)

    @pl.loop(0, rows // step)
    def _(block):
        at = block * step
        for c in range(chunks):
            out[pl.ds(at * chunks + c, step, stride=chunks), :] = base[
                pl.ds(pl.multiple_of(at, step), step), c * LANES:(c + 1) * LANES]


def pick_branch(pair_mask):
    live = jnp.sum((pair_mask[:2, 2:] > 0).astype(jnp.int32))
    branch = jnp.int32(0)
    for slots in (0, *SLOTS[:-1]):
        branch = branch + (live > slots).astype(jnp.int32)
    return branch


def opening(three_center, occ_energy, vir_energy, pair_mask):
    rows, _, virt = three_center.shape
    chunks = virt // LANES
    half = rows // 2
    z_count = lax.axis_size("aux") // 2
    pair = lax.axis_index("pair")
    side, lane = pair // 2, pair % 2
    own = three_center.reshape(rows * chunks, LANES)
    bf16, f32 = jnp.bfloat16, jnp.float32
    block_flops = 6 * rows * virt * virt
    flat_pieces = own.reshape(2, half * chunks, LANES)
    near = across(pick(flat_pieces, 1 - side), 0, 2)
    twin = across(own, 0, 1)
    split = [(rows, virt, bf16)] * 2
    mixed_rows, packed = virt // 2, packed_rows(chunks)
    keep_a, send_a, own_top, own_low = call(
        functools.partial(own_kernel, rows, chunks), [(packed // 2, virt)] * 2 + split, [own],
        scratch=[((virt, virt), f32)] * 2 + [((packed, virt), f32)], flops=block_flops)
    got_a = across(send_a, 1, 0)
    twin, send_a = lax.optimization_barrier((twin, send_a))
    keep_b, send_b, twin_top, twin_low = call(
        functools.partial(twin_kernel, rows, chunks), [(mixed_rows // 2, virt)] * 2 + split,
        [own_top, own_low, twin],
        scratch=[((mixed_rows, virt), f32), ((-(-chunks // 2) * LANES, virt), f32)],
        flops=block_flops)
    got_b = across(send_b, 1, 0)
    occ_energy, send_b = lax.optimization_barrier((occ_energy, send_b))
    got_a, later_mask = lax.optimization_barrier((got_a, pair_mask))
    branch = pick_branch(later_mask)
    occ_side = jnp.concatenate([occ_energy, across(occ_energy, 0, 1)])
    occ_side = jnp.where(lane == 0, occ_side, occ_side[::-1])
    occ_other = across(occ_side, 0, 2)
    occ = (occ_side, occ_other)
    later_own, _ = lax.optimization_barrier((own, send_b))
    far_send = pick(later_own.reshape(2, half * chunks, LANES), side)
    keep_a, branch, far_send = lax.optimization_barrier((keep_a, branch, far_send))
    piece_rows = (packed + mixed_rows) // 2 // z_count
    *pieces, vir_row, vir_col = call(
        x_add_kernel,
        [(piece_rows, virt)] * z_count + [(1, 2 * virt), (virt, LANES)],
        [vir_energy.reshape(1, virt), keep_a, got_a, keep_b, got_b])
    side_got = [across(pieces[s], s << 1, 0) for s in range(1, z_count)]
    near_t = across(near, 0, 1)
    most = SLOTS[-1] * mixed_rows
    cross = call(
        functools.partial(cross_kernel, half, chunks),
        [(n * mixed_rows // 4, virt) for n in SLOTS for _ in range(4)] + split,
        [pair_mask, own_top, own_low, twin_top, twin_low, near, near_t], in_smem=(0,),
        scratch=[((4, half, virt), bf16)] * 2 + [
            ((most, virt), f32), ((-(-chunks // 2) * LANES, virt), f32)],
        flops=block_flops)
    cross, faces = cross[:-2], cross[-2:]
    return lax.optimization_barrier((
        (own_top, own_low, twin_top, twin_low), faces, far_send, occ,
        [pieces[0], *side_got], cross, (vir_row, vir_col))), branch


def closing(slots, shape, opened, pair_mask):
    splits, faces, far_send, occ, side_parts, cross, virs = opened
    rows, _, virt = shape
    chunks = virt // LANES
    z_count = lax.axis_size("aux") // 2
    bf16, f32 = jnp.bfloat16, jnp.float32
    block_flops = 6 * rows * virt * virt
    energies = [pair_mask, *occ, *virs]
    piece_rows = side_parts[0].shape[0]
    own_size = own_share(piece_rows, chunks)
    total_rows = slots * virt // 2
    square_rows = total_rows // 4
    slab_rows = square_rows // z_count
    flips = [(0, 0), (1, 0), (0, 2), (1, 2)]

    def z_spread(slab, relay):
        got = {0: slab}
        for s in range(1, z_count):
            direct = s & (s - 1) == 0 or not relay
            got[s] = across(got[0 if direct else s & (s - 1)],
                           (s if direct else s & -s) << 1, 0)
        return [got[s] for s in range(1, z_count)]

    if slots:
        at = 4 * SLOTS.index(slots)
        cross = cross[at:at + 4]
        cross_got = [across(cross[s], *flips[s]) for s in range(1, 4)]
    slab, = call(
        functools.partial(scale_kernel, chunks, 0, z_count, True),
        [(piece_rows, virt)], [*energies, *side_parts], in_smem=(0, 1, 2))
    side_slabs = [slab] + z_spread(slab, False)
    joined, = call(
        functools.partial(join_kernel, (own_size, piece_rows - own_size)),
        [(piece_rows * z_count, virt)], side_slabs)
    other = across(joined, 1, 0)
    joined_t = across(joined, 0, 1)
    other_t = across(other, 0, 1)
    gamma, = call(
        functools.partial(near_gamma_kernel, rows, chunks), [(rows, virt)],
        [*splits, joined, other, joined_t, other_t],
        scratch=[((2, packed_rows(chunks) + virt // 2, virt), f32), ((virt, virt), f32),
                 ((2, 3 * virt, virt), bf16)], flops=2 * block_flops)
    if not slots:
        gamma, = call(functools.partial(flat_kernel, rows, chunks), [(rows * chunks, LANES)],
                      [gamma])
        return gamma
    if slots <= WHOLE_SLOTS:
        summed, = call(sum_kernel, [(square_rows, virt)], [cross[0], *cross_got])
        z_got = z_spread(summed, True)
        joined_c, = call(
            functools.partial(scale_kernel, chunks, slots, z_count, False),
            [(square_rows, virt)], [*energies, summed, *z_got], in_smem=(0, 1, 2))
    else:
        pieces_c = call(
            functools.partial(add_kernel, 4, 1), [(slab_rows, virt)] * z_count,
            [cross[0], *cross_got])
        summed = pieces_c[0]
        z_got = [across(pieces_c[s], s << 1, 0) for s in range(1, z_count)]
        cross_slab, = call(
            functools.partial(scale_kernel, chunks, slots, z_count, True),
            [(slab_rows, virt)], [*energies, pieces_c[0], *z_got], in_smem=(0, 1, 2))
        joined_c, = call(
            functools.partial(join_kernel, (slab_rows,)), [(square_rows, virt)],
            [cross_slab] + z_spread(cross_slab, False))
    far_send, summed = lax.optimization_barrier((far_send, summed))
    far = across(far_send, 0, 2)
    far_t = across(far, 0, 1)
    whole = [across(joined_c, *flips[s]) for s in range(1, 4)]
    joined_ct = across(joined_c, 0, 1)
    whole_t = [across(piece, 0, 1) for piece in whole]
    gamma, = call(
        functools.partial(far_gamma_kernel, rows, chunks, slots),
        [(rows * chunks, LANES)],
        [pair_mask, gamma, *faces, far, far_t, joined_c, *whole, joined_ct, *whole_t],
        in_smem=(0,),
        scratch=[((2, total_rows, virt), f32), ((virt, virt), f32),
                 ((3 * virt, virt), bf16), ((rows, virt), f32)],
        flops=2 * block_flops)
    return gamma


def on_device(three_center, occ_energy, vir_energy, pair_mask):
    rows, occ_count, virt = three_center.shape
    aux_count, pair_count = lax.axis_size("aux"), lax.axis_size("pair")
    z_count = aux_count // 2
    fits = (
        occ_count == 1 and pair_count == 4 and z_count in (2, 4) and aux_count == 2 * z_count
        and virt % LANES == 0 and rows % 16 == 0
        and virt // LANES % 2 == 1 and virt % (32 * z_count) == 0
        and packed_rows(virt // LANES) % (16 * z_count) == 0)
    args = (three_center, occ_energy, vir_energy, pair_mask)
    if not fits:
        return general_path(*args)
    opened, branch = opening(three_center, occ_energy, vir_energy, pair_mask)
    gamma = lax.switch(
        branch, [functools.partial(closing, n, three_center.shape)
                 for n in (0, *SLOTS)],
        opened, pair_mask)
    return gamma.reshape(three_center.shape)


def solution(mesh):
    in_specs = (P("aux", "pair", None), P("pair"), P(), P())
    out_specs = P("aux", "pair", None)
    return jax.shard_map(
        on_device, mesh=mesh, in_specs=in_specs, out_specs=out_specs, check_vma=False
    )
```

```python
import functools

import jax
import jax.numpy as jnp
from jax import lax
from jax.experimental import pallas as pl
from jax.experimental.pallas import tpu as pltpu
from jax.sharding import PartitionSpec as P

AXES = ("aux", "pair")
precision = lax.Precision.HIGH


def across(value, aux_flip, pair_flip):
    aux_count, pair_count = lax.axis_size("aux"), lax.axis_size("pair")
    moves = [
        (a * pair_count + p, (a ^ aux_flip) * pair_count + (p ^ pair_flip))
        for a in range(aux_count)
        for p in range(pair_count)
    ]
    return lax.ppermute(value, AXES, moves)


def pick(pieces, index):
    return lax.dynamic_index_in_dim(pieces, index, 0, keepdims=False)


def tn(left, right):
    return lax.dot_general(
        left, right, (((0,), (0,)), ((), ())), precision=precision,
        preferred_element_type=jnp.float32)


def nt(left, right):
    return lax.dot_general(
        left, right, (((1,), (1,)), ((), ())), precision=precision,
        preferred_element_type=jnp.float32)


def scatter_sum(value, flips, index):
    members = len(flips)
    pieces = value.reshape((members, value.shape[0] // members) + value.shape[1:])
    total = pick(pieces, index)
    for step in range(1, members):
        total = total + across(pick(pieces, index ^ step), *flips[step])
    return total


def gather(piece, flips, index):
    members = len(flips)
    whole = jnp.zeros((members,) + piece.shape, piece.dtype)
    whole = lax.dynamic_update_index_in_dim(whole, piece, index, 0)
    for step in range(1, members):
        whole = lax.dynamic_update_index_in_dim(
            whole, across(piece, *flips[step]), index ^ step, 0)
    return whole.reshape((members * piece.shape[0],) + piece.shape[1:])


def aux_groups(aux_count):
    bits = aux_count.bit_length() - 1
    low, groups = 1, []
    while low < bits:
        width = min(2, bits - low)
        groups.append((low, width))
        low += width
    return groups


def general_path(three_center, occ_energy, vir_energy, pair_mask):
    rows, occ_count, virt = three_center.shape
    aux_count = lax.axis_size("aux")
    aux, pair = lax.axis_index("aux"), lax.axis_index("pair")
    side, lane = pair // 2, pair % 2
    half = rows // 2
    own = three_center.reshape(rows, virt)
    pieces = own.reshape(2, half, virt)
    occ_side = jnp.stack([occ_energy[0], across(occ_energy, 0, 1)[0]])
    occ_side = jnp.where(lane == 0, occ_side, occ_side[::-1])
    occ_other = across(occ_side, 0, 2)
    occ_low = jnp.where(side == 0, occ_side, occ_other)
    occ_high = jnp.where(side == 0, occ_other, occ_side)
    mask = pair_mask.astype(jnp.float32)

    facing_near = across(pick(pieces, side ^ 1), 0, 2)
    twin = across(own, 0, 1)
    facing_far = across(pick(pieces, side), 0, 2)

    z_groups = aux_groups(aux_count)

    def z_scatter(value):
        start = jnp.int32(0)
        for low, width in z_groups:
            members = 1 << width
            index = (aux >> low) & (members - 1)
            value = scatter_sum(value, [(s << low, 0) for s in range(members)], index)
            start = start + index * value.shape[0]
        return value, start

    def z_gather(value):
        for low, width in reversed(z_groups):
            members = 1 << width
            index = (aux >> low) & (members - 1)
            value = gather(value, [(s << low, 0) for s in range(members)], index)
        return value

    first = jnp.where(lane == 0, own, twin)
    second = jnp.where(lane == 0, twin, own)
    near = virt // 2
    left = lax.dynamic_slice_in_dim(first, lane * near, near, 1)
    side_ints = jnp.concatenate([tn(own, own), tn(left, second)], 0)
    x_flips = [(0, 0), (1, 0)]
    x_index = aux & 1
    part = scatter_sum(side_ints, x_flips, x_index)
    start = x_index * part.shape[0]
    part, more = z_scatter(part)
    start = start + more
    row = start + jnp.arange(part.shape[0])
    in_own = row < virt
    a_index = jnp.where(in_own, row, row - virt + lane * near)
    occ_i = jnp.where(in_own, pick(occ_side, lane), occ_side[0])
    occ_j = jnp.where(in_own, pick(occ_side, lane), occ_side[1])
    weight = jnp.where(
        in_own, mask[pair, pair], mask[2 * side, 2 * side + 1])
    row_term = jnp.take(vir_energy, a_index) - occ_i - occ_j
    part = weight[:, None] * part / (row_term[:, None] + vir_energy[None, :])
    side_amps = gather(z_gather(part), x_flips, x_index)
    own_amps = side_amps[:virt]
    mixed = side_amps[virt:]
    mixed_twin = across(mixed, 0, 1)
    mixed_amps = jnp.concatenate(
        [jnp.where(lane == 0, mixed, mixed_twin), jnp.where(lane == 0, mixed_twin, mixed)], 0)

    here = pick(pieces, side)
    twin_here = pick(twin.reshape(2, half, virt), side)
    facing_twin = across(facing_near, 0, 1)
    low = jnp.where(side == 0, here, facing_near)
    high = jnp.where(side == 0, facing_near, here)
    high_twin = jnp.where(side == 0, facing_twin, twin_here)
    high_first = jnp.where(lane == 0, high, high_twin)
    high_second = jnp.where(lane == 0, high_twin, high)
    cross_ints = jnp.concatenate([tn(low, high_first), tn(low, high_second)], 0)
    q_flips = [(0, 0), (1, 0), (0, 2), (1, 2)]
    q_index = (aux & 1) + 2 * side
    part = scatter_sum(cross_ints, q_flips, q_index)
    start = q_index * part.shape[0]
    part, more = z_scatter(part)
    start = start + more
    row = start + jnp.arange(part.shape[0])
    block = row // virt
    a_index = row % virt
    weight = jnp.where(block == 0, mask[lane, 2], mask[lane, 3])
    row_term = jnp.take(vir_energy, a_index) - pick(occ_low, lane) - jnp.where(
        block == 0, occ_high[0], occ_high[1])
    part = weight[:, None] * part / (row_term[:, None] + vir_energy[None, :])
    cross_amps = gather(z_gather(part), q_flips, q_index)

    cross_blocks = cross_amps.reshape(2, virt, virt)
    swapped = across(pick(cross_blocks, lane ^ 1), 0, 1)
    kept = pick(cross_blocks, lane)
    facing_far_twin = across(facing_far, 0, 1)
    zero_near = jnp.where(side == 0, facing_near, facing_far)
    zero_far = jnp.where(side == 0, facing_far, facing_near)
    facing = jnp.concatenate([zero_near, zero_far], 0)
    twin_near = jnp.where(side == 0, facing_twin, facing_far_twin)
    twin_far = jnp.where(side == 0, facing_far_twin, facing_twin)
    facing_t = jnp.concatenate([twin_near, twin_far], 0)
    f_first = jnp.where(lane == 0, facing, facing_t)
    f_second = jnp.where(lane == 0, facing_t, facing)
    low_amps = jnp.where(lane == 0, kept, swapped)
    high_amps = jnp.where(lane == 0, swapped, kept)
    m0 = jnp.where(side == 0, cross_blocks[0], low_amps.T)
    m1 = jnp.where(side == 0, cross_blocks[1], high_amps.T)
    mixed_use = jnp.where(lane == 0, mixed_amps, mixed_amps.T)
    gamma = nt(own, own_amps) + nt(twin, mixed_use) + nt(f_first, m0) + nt(f_second, m1)
    return gamma.reshape(rows, occ_count, virt)


LANES = 128
IN_VMEM = pl.BlockSpec(memory_space=pltpu.VMEM)
IN_SMEM = pl.BlockSpec(memory_space=pltpu.SMEM)
SLOTS = (1, 2, 4)
WHOLE_SLOTS = 4
STEP = 1024
SPARE_BYTES = 2 << 20


def dot_tn(left, right):
    return lax.dot_general(
        left, right, (((0,), (0,)), ((), ())), preferred_element_type=jnp.float32)


def dot_nn(left, right):
    return jnp.dot(left, right, preferred_element_type=jnp.float32)


def halves(value):
    top = value.astype(jnp.bfloat16)
    return top, (value - top.astype(jnp.float32)).astype(jnp.bfloat16)


def spots():
    aux, pair = lax.axis_index("aux"), lax.axis_index("pair")
    return aux & 1, aux >> 1, pair >> 1, pair & 1, pair


def call(kernel, outs, args, in_smem=(), scratch=(), flops=0):
    outs = [jax.ShapeDtypeStruct(o[:2], o[2] if len(o) > 2 else jnp.float32) for o in outs]
    scratch = [jax.ShapeDtypeStruct(*s) for s in scratch]
    moved = sum(a.size * a.dtype.itemsize for a in (*args, *outs))
    held = moved + sum(s.size * s.dtype.itemsize for s in scratch)
    return pl.pallas_call(
        kernel,
        out_shape=outs,
        in_specs=[IN_SMEM if i in in_smem else IN_VMEM for i in range(len(args))],
        out_specs=[IN_VMEM for _ in outs],
        scratch_shapes=[pltpu.VMEM(s.shape, s.dtype) for s in scratch],
        cost_estimate=pl.CostEstimate(flops=flops, bytes_accessed=moved, transcendentals=0),
        compiler_params=pltpu.CompilerParams(vmem_limit_bytes=held + SPARE_BYTES),
    )(*args)


def unpack(ref, rows, chunks, top_ref, low_ref):
    step = min(256, rows)

    @pl.loop(0, rows // step)
    def _(block):
        for c in range(chunks):
            top, low = halves(ref[pl.ds(block * step * chunks + c, step, stride=chunks), :])
            where = pl.ds(pl.multiple_of(block * step, step), step)
            top_ref[where, c * LANES:(c + 1) * LANES] = top
            low_ref[where, c * LANES:(c + 1) * LANES] = low


def half_rows(left, right, lane, chunks, spare):
    virt = chunks * LANES
    width = -(-chunks // 2) * LANES
    begin = lane * (chunks // 2) * LANES
    where = pl.ds(pl.multiple_of(begin, LANES), width)
    lt, ll = left[0][:, where], left[1][:, where]
    rt, rl = right[0][...], right[1][...]
    spare[...] = (dot_tn(rt, lt) + (dot_tn(rt, ll) + dot_tn(rl, lt))).T
    skip = lane * (virt // 2) - begin
    return spare[pl.ds(pl.multiple_of(skip, 8), virt // 2), :]


def packed_rows(chunks):
    return (chunks + 1) // 2 * LANES


def own_share(size, chunks):
    packed = packed_rows(chunks)
    return size * packed // (packed + chunks * LANES // 2)


def triangle_parts(chunks):
    for r in range((chunks + 1) // 2):
        yield r, 0, r
        if r:
            yield r, (chunks - r) * LANES, chunks - r


def own_kernel(rows, chunks, own, keep, send, far, top, low, acc, cross, packed):
    x, _, side, _, _ = spots()
    count = far.shape[0]
    far[...] = own[pl.ds(pl.multiple_of(side * count, 8), count), :]
    unpack(own, rows, chunks, top, low)
    cross[...] = dot_tn(top[...], low[...])
    acc[...] = dot_tn(top[...], top[...]) + (cross[...] + cross[...].T)
    for r, column, block in triangle_parts(chunks):
        width = (chunks - block) * LANES
        packed[r * LANES:(r + 1) * LANES, column:column + width] = acc[
            block * LANES:(block + 1) * LANES, block * LANES:]
    size = keep.shape[0]
    keep[...] = packed[pl.ds(pl.multiple_of(x * size, 8), size), :]
    send[...] = packed[pl.ds(pl.multiple_of((1 - x) * size, 8), size), :]


def twin_kernel(rows, chunks, own_top, own_low, twin, keep, send, top, low, acc, spare):
    x, _, _, lane, _ = spots()
    unpack(twin, rows, chunks, top, low)
    own, other = (own_top, own_low), (top, low)
    for here, left, right in ((0, own, other), (1, other, own)):

        @pl.when(lane == here)
        def _(here=here, left=left, right=right):
            acc[...] = half_rows(left, right, here, chunks, spare)

    size = keep.shape[0]
    keep[...] = acc[pl.ds(pl.multiple_of(x * size, 8), size), :]
    send[...] = acc[pl.ds(pl.multiple_of((1 - x) * size, 8), size), :]


def side_pair(mask, slot, slots):
    if slots == 4:
        return slot // 2, 2 + slot % 2, mask[slot // 2, 2 + slot % 2]
    count, found, weight = jnp.int32(0), jnp.int32(0), jnp.int32(0)
    for k in range(4):
        live = mask[k // 2, 2 + k % 2]
        hit = (live > 0) & (count == slot)
        found = jnp.where(hit, k, found)
        weight = jnp.where(hit, live, weight)
        count = count + (live > 0).astype(jnp.int32)
    return found // 2, 2 + found % 2, weight


def cross_kernel(half, chunks, mask, own_top, own_low, twin_top, twin_low, face, face_twin,
                 *rest):
    outs, (face_tops, face_lows), (top, low, acc, spare) = rest[:-6], rest[-6:-4], rest[-4:]
    x, _, side, lane, pair = spots()
    virt = chunks * LANES
    rows = pl.ds(pl.multiple_of(side * half, half), half)
    top[pair], low[pair] = own_top[rows, :], own_low[rows, :]
    top[pair ^ 1], low[pair ^ 1] = twin_top[rows, :], twin_low[rows, :]
    for ref, flip in ((face, 2), (face_twin, 3)):
        which = pair ^ flip
        unpack(ref, half, chunks, top.at[which], low.at[which])
        at = slice((flip - 2) * half, (flip - 1) * half)
        face_tops[at, :], face_lows[at, :] = top[which], low[which]
    live = jnp.int32(0)
    for k in range(4):
        live = live + (mask[k // 2, 2 + k % 2] > 0).astype(jnp.int32)
    square = x + 2 * side
    for number, slots in enumerate(SLOTS):
        fewer = SLOTS[number - 1] if number else 0

        @pl.when((live > fewer) & (live <= slots))
        def _(number=number, slots=slots):
            for slot in range(slots):
                first, second, _ = side_pair(mask, slot, slots)
                acc[slot * virt // 2:(slot + 1) * virt // 2, :] = half_rows(
                    (top.at[first], low.at[first]), (top.at[second], low.at[second]),
                    lane, chunks, spare)
            mine = outs[4 * number:4 * number + 4]
            size = mine[0].shape[0]
            for step in range(4):
                mine[step][...] = acc[
                    pl.ds(pl.multiple_of((square ^ step) * size, 8), size), :]


def add_kernel(members, sets, *refs):
    _, z, _, _, _ = spots()
    ins, outs = refs[:members * sets], refs[members * sets:]
    count = len(outs)
    at = 0
    for which in range(sets):
        mine = ins[which * members:(which + 1) * members]
        size = mine[0].shape[0] // count
        for step in range(count):
            where = pl.ds(pl.multiple_of((z ^ step) * size, 8), size)
            total = mine[0][where, :]
            for other in mine[1:]:
                total = total + other[where, :]
            outs[step][at:at + size, :] = total
        at += size


def x_add_kernel(vir, *refs):
    vir_row, vir_col = refs[-2:]
    virt = vir.shape[1]
    vir_row[:, :virt] = vir[...]
    vir_row[:, virt:] = vir[...]
    vir_col[...] = jnp.broadcast_to(vir[...], (LANES, virt)).T
    add_kernel(2, 2, *refs[:-2])


def sum_kernel(*refs):
    total = refs[0][...]
    for other in refs[1:-1]:
        total = total + other[...]
    refs[-1][...] = total


def join_kernel(sizes, *refs):
    _, z, _, _, _ = spots()
    out, ins = refs[-1], refs[:-1]
    inner = outer = 0
    for size in sizes:
        for step, piece in enumerate(ins):
            at = pl.multiple_of(outer + (z ^ step) * size, 8)
            out[pl.ds(at, size), :] = piece[inner:inner + size, :]
        inner += size
        outer += size * len(ins)


def scale_kernel(chunks, slots, members, cut, mask, occ_side, occ_other, vir_row, vir_col,
                 *refs):
    x, z, side, lane, pair = spots()
    ins, out = refs[:members], refs[members]

    def occ(which):
        mine, lane_of = (which >> 1) == side, which & 1
        return jnp.where(mine, occ_side[lane_of], occ_other[lane_of])

    virt = chunks * LANES
    size = out.shape[0]
    own_size = own_share(size, chunks)
    lanes = lax.broadcasted_iota(jnp.int32, (8, virt), 1)
    for group in range(size // 8):
        row = group * 8
        packed = slots == 0 and row < own_size
        if packed:
            row = (x * members + z) * own_size + row
            tile, inner = row >> (LANES.bit_length() - 1), row & (LANES - 1)
            first = second = pair
            weight = mask[pair, pair]
        elif slots == 0:
            row = (x * members + z) * (size - own_size) + row - own_size
            first, second = 2 * side, 2 * side + 1
            weight = mask[first, second]
            origin = lane * (virt // 2) + row
        else:
            row = ((x + 2 * side) * (members if cut else 1) + (z if cut else 0)) * size + row
            first, second, weight = side_pair(mask, 0, slots)
            inner = row
            for slot in range(1, slots):
                f, s, w = side_pair(mask, slot, slots)
                here = row >= slot * (virt // 2)
                first = jnp.where(here, f, first)
                second = jnp.where(here, s, second)
                weight = jnp.where(here, w, weight)
                inner = jnp.where(here, row - slot * (virt // 2), inner)
            origin = lane * (virt // 2) + inner
        here = slice(group * 8, group * 8 + 8)
        total = ins[0][here, :]
        for other in ins[1:]:
            total = total + other[here, :]
        if packed:
            ahead = pl.multiple_of(tile * LANES, LANES)
            behind = jnp.minimum(virt - tile * LANES, virt - LANES)
            energy = jnp.where(
                lanes < virt - tile * LANES,
                vir_col[pl.ds(pl.multiple_of(ahead + inner, 8), 8), 0:1]
                + vir_row[:, pl.ds(ahead, virt)],
                vir_col[pl.ds(pl.multiple_of(behind + inner, 8), 8), 0:1] + vir_row[:, :virt])
        else:
            energy = vir_col[pl.ds(pl.multiple_of(origin, 8), 8), 0:1] + vir_row[:, :virt]
        energy = energy - occ(first) - occ(second)
        out[here, :] = weight.astype(jnp.float32) * total / energy


def place_block(halves_ref, first, chunks, whole):
    part = chunks * LANES // 2
    for lane in range(2):
        whole[lane * part:(lane + 1) * part, :] = halves_ref[lane, pl.ds(first, part), :]


def wide(top, low):
    return jnp.concatenate([top, low, top], 1)


def stack(value, stacked):
    virt = value.shape[0]
    top, low = halves(value)
    stacked[0:virt, :] = top
    stacked[virt:2 * virt, :] = top
    stacked[2 * virt:3 * virt, :] = low


def near_gamma_kernel(rows, chunks, own_top, own_low, twin_top, twin_low,
                      keep, other, keep_t, other_t, out, parts, whole, stacked):
    x, _, _, lane, _ = spots()
    size = keep.shape[0]
    own_size = own_share(size, chunks)
    mixed = size - own_size
    mixed_start = packed_rows(chunks)
    for ref, slot, piece in ((keep, lane, x), (other, lane, 1 - x),
                             (keep_t, 1 - lane, x), (other_t, 1 - lane, 1 - x)):
        parts[slot, pl.ds(pl.multiple_of(piece * own_size, 8), own_size), :] = ref[:own_size, :]
        parts[slot, pl.ds(pl.multiple_of(mixed_start + piece * mixed, 8), mixed), :] = ref[own_size:, :]
    for r, column, block in triangle_parts(chunks):
        for other_block in range(block, chunks):
            at = column + (other_block - block) * LANES
            tile = parts[lane, r * LANES:(r + 1) * LANES, at:at + LANES]
            mine, theirs = (slice(b * LANES, (b + 1) * LANES) for b in (block, other_block))
            whole[mine, theirs] = tile
            if other_block != block:
                whole[theirs, mine] = tile.T
    stack(whole[...], stacked.at[0])
    place_block(parts, mixed_start, chunks, whole)

    @pl.when(lane == 0)
    def _():
        stack(whole[...].T, stacked.at[1])

    @pl.when(lane == 1)
    def _():
        stack(whole[...], stacked.at[1])

    step = min(STEP, rows)

    @pl.loop(0, rows // step)
    def _(block):
        at = pl.ds(pl.multiple_of(block * step, step), step)
        out[at, :] = dot_nn(wide(own_top[at, :], own_low[at, :]), stacked[0]) + dot_nn(
            wide(twin_top[at, :], twin_low[at, :]), stacked[1])


def far_gamma_kernel(rows, chunks, slots, mask, base, face_tops, face_lows, far, far_t, *rest):
    pieces, pieces_t = rest[0:4], rest[4:8]
    out, parts, whole, stacked, total = rest[8:]
    x, _, side, lane, pair = spots()
    virt = chunks * LANES
    half = rows // 2
    size = pieces[0].shape[0]
    square = x + 2 * side
    for step in range(4):
        where = pl.ds(pl.multiple_of((square ^ step) * size, 8), size)
        parts[lane, where, :] = pieces[step][...]
        parts[1 - lane, where, :] = pieces_t[step][...]
    step = min(STEP, half)
    total[...] = base[...]
    for flip in (0, 1):
        partner = pair ^ (2 + flip)
        first = jnp.minimum(pair, partner)
        second = jnp.maximum(pair, partner)
        live, at = jnp.int32(0), jnp.int32(0)
        for slot in range(slots):
            f, s, weight = side_pair(mask, slot, slots)
            hit = (f == first) & (s == second) & (weight > 0)
            live = jnp.where(hit, 1, live)
            at = jnp.where(hit, slot, at)

        @pl.when(live > 0)
        def _(flip=flip, at=at):
            place_block(parts, pl.multiple_of(at * (virt // 2), 8), chunks, whole)

            @pl.when(side == 0)
            def _():
                stack(whole[...].T, stacked)

            @pl.when(side == 1)
            def _():
                stack(whole[...], stacked)

            @pl.loop(0, half // step)
            def _(block):
                rows_in = pl.ds(pl.multiple_of(flip * half + block * step, step), step)
                rows_out = pl.ds(pl.multiple_of(side * half + block * step, step), step)
                total[rows_out, :] += dot_nn(
                    wide(face_tops[rows_in, :], face_lows[rows_in, :]), stacked[...])
                source = far_t if flip else far
                parts_in = [
                    halves(source[pl.ds(block * step * chunks + c, step, stride=chunks), :])
                    for c in range(chunks)]
                tops, lows = [p[0] for p in parts_in], [p[1] for p in parts_in]
                rows_out = pl.ds(pl.multiple_of((1 - side) * half + block * step, step), step)
                total[rows_out, :] += dot_nn(
                    jnp.concatenate(tops + lows + tops, 1), stacked[...])

    flat_kernel(rows, chunks, total, out)


def flat_kernel(rows, chunks, base, out):
    step = min(256, rows)

    @pl.loop(0, rows // step)
    def _(block):
        at = block * step
        for c in range(chunks):
            out[pl.ds(at * chunks + c, step, stride=chunks), :] = base[
                pl.ds(pl.multiple_of(at, step), step), c * LANES:(c + 1) * LANES]


def pick_branch(pair_mask):
    live = jnp.sum((pair_mask[:2, 2:] > 0).astype(jnp.int32))
    branch = jnp.int32(0)
    for slots in (0, *SLOTS[:-1]):
        branch = branch + (live > slots).astype(jnp.int32)
    return branch


def opening(three_center, occ_energy, vir_energy, pair_mask):
    rows, _, virt = three_center.shape
    chunks = virt // LANES
    half = rows // 2
    z_count = lax.axis_size("aux") // 2
    pair = lax.axis_index("pair")
    side, lane = pair // 2, pair % 2
    own = three_center.reshape(rows * chunks, LANES)
    bf16, f32 = jnp.bfloat16, jnp.float32
    block_flops = 6 * rows * virt * virt
    flat_pieces = own.reshape(2, half * chunks, LANES)
    near = across(pick(flat_pieces, 1 - side), 0, 2)
    twin = across(own, 0, 1)
    split = [(rows, virt, bf16)] * 2
    mixed_rows, packed = virt // 2, packed_rows(chunks)
    keep_a, send_a, far_send, own_top, own_low = call(
        functools.partial(own_kernel, rows, chunks),
        [(packed // 2, virt)] * 2 + [(half * chunks, LANES)] + split, [own],
        scratch=[((virt, virt), f32)] * 2 + [((packed, virt), f32)], flops=block_flops)
    got_a = across(send_a, 1, 0)
    twin, send_a = lax.optimization_barrier((twin, send_a))
    keep_b, send_b, twin_top, twin_low = call(
        functools.partial(twin_kernel, rows, chunks), [(mixed_rows // 2, virt)] * 2 + split,
        [own_top, own_low, twin],
        scratch=[((mixed_rows, virt), f32), ((-(-chunks // 2) * LANES, virt), f32)],
        flops=block_flops)
    got_b = across(send_b, 1, 0)
    occ_energy, send_b = lax.optimization_barrier((occ_energy, send_b))
    got_a, later_mask = lax.optimization_barrier((got_a, pair_mask))
    branch = pick_branch(later_mask)
    occ_side = jnp.concatenate([occ_energy, across(occ_energy, 0, 1)])
    occ_side = jnp.where(lane == 0, occ_side, occ_side[::-1])
    occ_other = across(occ_side, 0, 2)
    occ = (occ_side, occ_other)
    piece_rows = (packed + mixed_rows) // 2 // z_count
    *pieces, vir_row, vir_col = call(
        x_add_kernel,
        [(piece_rows, virt)] * z_count + [(1, 2 * virt), (virt, LANES)],
        [vir_energy.reshape(1, virt), keep_a, got_a, keep_b, got_b])
    side_got = [across(pieces[s], s << 1, 0) for s in range(1, z_count)]
    near_t = across(near, 0, 1)
    most = SLOTS[-1] * mixed_rows
    cross = call(
        functools.partial(cross_kernel, half, chunks),
        [(n * mixed_rows // 4, virt) for n in SLOTS for _ in range(4)] + split,
        [pair_mask, own_top, own_low, twin_top, twin_low, near, near_t], in_smem=(0,),
        scratch=[((4, half, virt), bf16)] * 2 + [
            ((most, virt), f32), ((-(-chunks // 2) * LANES, virt), f32)],
        flops=block_flops)
    cross, faces = cross[:-2], cross[-2:]
    return lax.optimization_barrier((
        (own_top, own_low, twin_top, twin_low), faces, far_send, occ,
        [pieces[0], *side_got], cross, (vir_row, vir_col))), branch


def closing(slots, shape, opened, pair_mask):
    splits, faces, far_send, occ, side_parts, cross, virs = opened
    rows, _, virt = shape
    chunks = virt // LANES
    z_count = lax.axis_size("aux") // 2
    bf16, f32 = jnp.bfloat16, jnp.float32
    block_flops = 6 * rows * virt * virt
    energies = [pair_mask, *occ, *virs]
    piece_rows = side_parts[0].shape[0]
    own_size = own_share(piece_rows, chunks)
    total_rows = slots * virt // 2
    square_rows = total_rows // 4
    slab_rows = square_rows // z_count
    flips = [(0, 0), (1, 0), (0, 2), (1, 2)]

    def z_spread(slab, relay):
        got = {0: slab}
        for s in range(1, z_count):
            direct = s & (s - 1) == 0 or not relay
            got[s] = across(got[0 if direct else s & (s - 1)],
                           (s if direct else s & -s) << 1, 0)
        return [got[s] for s in range(1, z_count)]

    if slots:
        at = 4 * SLOTS.index(slots)
        cross = cross[at:at + 4]
        cross_got = [across(cross[s], *flips[s]) for s in range(1, 4)]
    slab, = call(
        functools.partial(scale_kernel, chunks, 0, z_count, True),
        [(piece_rows, virt)], [*energies, *side_parts], in_smem=(0, 1, 2))
    side_slabs = [slab] + z_spread(slab, False)
    joined, = call(
        functools.partial(join_kernel, (own_size, piece_rows - own_size)),
        [(piece_rows * z_count, virt)], side_slabs)
    other = across(joined, 1, 0)
    joined_t = across(joined, 0, 1)
    other_t = across(other, 0, 1)
    gamma, = call(
        functools.partial(near_gamma_kernel, rows, chunks), [(rows, virt)],
        [*splits, joined, other, joined_t, other_t],
        scratch=[((2, packed_rows(chunks) + virt // 2, virt), f32), ((virt, virt), f32),
                 ((2, 3 * virt, virt), bf16)], flops=2 * block_flops)
    if not slots:
        gamma, = call(functools.partial(flat_kernel, rows, chunks), [(rows * chunks, LANES)],
                      [gamma])
        return gamma
    if slots <= WHOLE_SLOTS:
        summed, = call(sum_kernel, [(square_rows, virt)], [cross[0], *cross_got])
        z_got = z_spread(summed, True)
        joined_c, = call(
            functools.partial(scale_kernel, chunks, slots, z_count, False),
            [(square_rows, virt)], [*energies, summed, *z_got], in_smem=(0, 1, 2))
    else:
        pieces_c = call(
            functools.partial(add_kernel, 4, 1), [(slab_rows, virt)] * z_count,
            [cross[0], *cross_got])
        summed = pieces_c[0]
        z_got = [across(pieces_c[s], s << 1, 0) for s in range(1, z_count)]
        cross_slab, = call(
            functools.partial(scale_kernel, chunks, slots, z_count, True),
            [(slab_rows, virt)], [*energies, pieces_c[0], *z_got], in_smem=(0, 1, 2))
        joined_c, = call(
            functools.partial(join_kernel, (slab_rows,)), [(square_rows, virt)],
            [cross_slab] + z_spread(cross_slab, False))
    far_send, summed = lax.optimization_barrier((far_send, summed))
    far = across(far_send, 0, 2)
    far_t = across(far, 0, 1)
    whole = [across(joined_c, *flips[s]) for s in range(1, 4)]
    joined_ct = across(joined_c, 0, 1)
    whole_t = [across(piece, 0, 1) for piece in whole]
    gamma, = call(
        functools.partial(far_gamma_kernel, rows, chunks, slots),
        [(rows * chunks, LANES)],
        [pair_mask, gamma, *faces, far, far_t, joined_c, *whole, joined_ct, *whole_t],
        in_smem=(0,),
        scratch=[((2, total_rows, virt), f32), ((virt, virt), f32),
                 ((3 * virt, virt), bf16), ((rows, virt), f32)],
        flops=2 * block_flops)
    return gamma


def on_device(three_center, occ_energy, vir_energy, pair_mask):
    rows, occ_count, virt = three_center.shape
    aux_count, pair_count = lax.axis_size("aux"), lax.axis_size("pair")
    z_count = aux_count // 2
    fits = (
        occ_count == 1 and pair_count == 4 and z_count in (2, 4) and aux_count == 2 * z_count
        and virt % LANES == 0 and rows % 16 == 0
        and virt // LANES % 2 == 1 and virt % (32 * z_count) == 0
        and packed_rows(virt // LANES) % (16 * z_count) == 0)
    args = (three_center, occ_energy, vir_energy, pair_mask)
    if not fits:
        return general_path(*args)
    opened, branch = opening(three_center, occ_energy, vir_energy, pair_mask)
    gamma = lax.switch(
        branch, [functools.partial(closing, n, three_center.shape)
                 for n in (0, *SLOTS)],
        opened, pair_mask)
    return gamma.reshape(three_center.shape)


def solution(mesh):
    in_specs = (P("aux", "pair", None), P("pair"), P(), P())
    out_specs = P("aux", "pair", None)
    return jax.shard_map(
        on_device, mesh=mesh, in_specs=in_specs, out_specs=out_specs, check_vma=False
    )
```
